512 devices in a mesh: group: 4 (over y_lo, core), dp: 8 (over y_hi, x), mp: 16 (over z).
Axes of the slice: x: 4, y: 4 (y_hi: 2, y_lo: 2; y = y_hi * 2 + y_lo), z: 16, core: 2. Of those that a mesh axis runs over, the one named last changes fastest.
Arguments:
- audio_states: bfloat16 [4, 4096, 1280], P('group', ('dp', 'mp')), may hold values from -6 to 6
- image_states: bfloat16 [4, 4096, 3200], P('group', ('dp', 'mp')), may hold values from -6 to 6
- audio_gain: float32 [1280], replicated, may hold values from 0.1 to 1.9
- image_gain: float32 [3200], replicated, may hold values from 0.1 to 1.9
- audio_proj: bfloat16 [1280, 8192], P('dp', 'mp'), may hold values from -1 to 1
- image_proj: bfloat16 [3200, 8192], P('dp', 'mp'), may hold values from -1 to 1
- block_rows: int32 [2, 8, 4], replicated, may hold values from 1 to 128
- destination: int32 [2, 8, 4], replicated, may hold values from 0 to 15, as said below
- input_gain: float32 [8192], P('mp'), may hold values from 0.1 to 1.9
- kv_weight: bfloat16 [8192, 2048], P('mp'), may hold values from -0.09375 to 0.09375
Outputs:
- key_values: bfloat16 [4, 4096, 2048], P('group', 'dp', 'mp')
- backbone_rows: bfloat16 [4, 4096, 8192], P('group', 'dp', 'mp')
The draws below stay inside these ranges and needn't reach their ends.
Inputs may be any that keep to these rules, and one draw needn't show every extreme that they name: `destination`: every backbone device receives exactly 2 blocks of each stream; an encoder index of dp sends either none or exactly 1 block of its stream to a backbone device.
All inputs are finite; a program needn't handle non-finite values.
Results may differ from the reference program's by a relative error of at most 0.012.
Values may be sent and summed in bfloat16 or wider, within the bound.
A program may use at most 64 MiB of HBM per device.

```python
import jax
import jax.numpy as jnp
from jax import lax

AUDIO_WIDTH = 1280
IMAGE_WIDTH = 3200
MODEL_WIDTH = 8192
KV_WIDTH = 2048
BLOCK = 128
BLOCKS = 4
CAPACITY = 1
ROWS = 4096
N_DP = 8
N_MP = 16


def column_scaled(key, row_count, col_count):
    base_key, scale_key = jax.random.split(key)
    raw_values = jnp.clip(jax.random.normal(base_key, (row_count, col_count), jnp.float32), -5.0, 5.0)
    scales = jnp.exp(jax.random.uniform(scale_key, (col_count,), jnp.float32, 0.0, jnp.log(10.0)))
    return jnp.clip(raw_values * scales[None, :] / (4.0 * jnp.sqrt(row_count * 1.0)), -1.0, 1.0)


def draw_audio_proj(key, part):
    return column_scaled(jax.random.fold_in(key, 3), AUDIO_WIDTH, MODEL_WIDTH).astype(jnp.bfloat16)


def draw_image_proj(key, part):
    return column_scaled(jax.random.fold_in(key, 4), IMAGE_WIDTH, MODEL_WIDTH).astype(jnp.bfloat16)


def stream_routes(key):
    dest_count = 2 * N_DP
    groups_each = BLOCKS // CAPACITY
    half_count = groups_each // 2
    keys = jax.random.split(key, 5)
    spread_order = jax.random.permutation(keys[0], N_DP)
    even_offsets = jax.random.permutation(keys[1], N_DP)[:half_count] * 2
    odd_offsets = jax.random.permutation(keys[2], N_DP)[:half_count] * 2 + 1
    offsets = jax.random.permutation(keys[3], jnp.concatenate([even_offsets, odd_offsets]))
    targets = (2 * spread_order[:, None] + offsets[None, :]) % dest_count
    rotation = dest_count - targets[N_DP - 1, 0]
    targets = (targets + rotation) % dest_count
    block_keys = jax.random.split(keys[4], N_DP)
    orders = jax.vmap(lambda one_key: jax.random.permutation(one_key, BLOCKS))(block_keys)
    return jnp.take_along_axis(targets, orders // CAPACITY, axis=1).astype(jnp.int32)


def draw_destination(key, part):
    base_key = jax.random.fold_in(key, 7)
    return jnp.stack([stream_routes(jax.random.fold_in(base_key, 0)), stream_routes(jax.random.fold_in(base_key, 1))])


def place_ends(values, own_key, smallest, largest):
    longest = values.shape.index(max(values.shape))
    spots = []
    for shift in (0, 1):
        where = [jax.random.randint(jax.random.fold_in(own_key, axis), (), 0, length) for axis, length in enumerate(values.shape)]
        where[longest] = (where[longest] + shift) % values.shape[longest]
        spots.append(tuple(where))
    return values.at[spots[0]].set(smallest).at[spots[1]].set(largest)


def with_spikes(values, key, source, target, blocks, factor):
    owner, partner = [(jnp.arange(values.shape[dim]) // (values.shape[dim] // blocks)).reshape([-1 if axis == dim else 1 for axis in range(values.ndim)]) for dim in (source, target)]
    chosen = jax.random.permutation(key, blocks)[partner]
    strong = (owner == chosen) | (owner == (partner + blocks // 2) % blocks)
    return jnp.where(strong, factor * values, values)


def block_levels(own_key, shape, cuts, smallest, high):
    level, own = 1.0, jax.random.fold_in(own_key, 6)
    for dim, parts in cuts:
        heights = jnp.exp(jax.random.uniform(jax.random.fold_in(own, dim), (parts,), jnp.float32, smallest / len(cuts), high / len(cuts)))
        level = level * jnp.repeat(heights, shape[dim] // parts).reshape([-1 if axis == dim else 1 for axis in range(len(shape))])
    return level


def bell_draw(own_key, dims, scale, most, shards=(), kind=jnp.bfloat16):
    values = jax.random.normal(own_key, dims, jnp.float32) * scale
    if len(shards) > 0:
        values = block_levels(own_key, dims, shards, -0.22, 0.18) * values
    return jnp.clip(values, min=-most, max=most).astype(kind)


def gaussian_with(stream_key, extent, width, limit, shards, heavy, kind=jnp.bfloat16):
    array = width * jax.random.normal(stream_key, extent, jnp.float32)
    if shards:
        array = array * block_levels(stream_key, extent, shards, -0.22, 0.18)
    return jnp.clip(with_spikes(array, jax.random.fold_in(stream_key, 3), *heavy), -limit, limit).astype(kind)


def setup_inputs(seed: int = 0) -> dict:
    streams_of = jax.random.split(jax.random.key(seed), 11)
    return {
        "audio_states": bell_draw(streams_of[0], (4, ROWS, AUDIO_WIDTH), 1.0, 6.0, ((0, 4), (1, 128))),
        "image_states": bell_draw(streams_of[1], (4, ROWS, IMAGE_WIDTH), 1.0, 6.0, ((0, 4), (1, 128))),
        "audio_gain": jnp.clip(1.0 + 0.18 * jax.random.normal(streams_of[2], (AUDIO_WIDTH,), jnp.float32), 0.1, 1.9),
        "image_gain": jnp.clip(1.0 + 0.18 * jax.random.normal(streams_of[3], (IMAGE_WIDTH,), jnp.float32), 0.1, 1.9),
        "audio_proj": draw_audio_proj(jax.random.fold_in(streams_of[10], 71), 0),
        "image_proj": draw_image_proj(jax.random.fold_in(streams_of[10], 71), 0),
        "block_rows": place_ends(jax.random.randint(streams_of[6], (2, N_DP, BLOCKS), 1, BLOCK + 1), jax.random.fold_in(streams_of[6], 1), 1, BLOCK).astype(jnp.int32),
        "destination": draw_destination(jax.random.fold_in(streams_of[10], 71), 0),
        "input_gain": jnp.clip(1.0 + 0.18 * jax.random.normal(streams_of[8], (MODEL_WIDTH,), jnp.float32), 0.1, 1.9),
        "kv_weight": gaussian_with(streams_of[9], (MODEL_WIDTH, KV_WIDTH), MODEL_WIDTH ** -0.5, 0.09375, ((0, 16),), (0, 1, 16, 2.0)),
    }


EPS_LAYER = 1e-05
EPS_ROOT = 1e-06

def layer_norm(values_in, gain_vec):
    values = values_in.astype(jnp.float32)
    center = values - lax.optimization_barrier(jnp.mean(values, axis=-1, keepdims=True))
    spread = lax.optimization_barrier(jnp.mean(center * center, axis=-1, keepdims=True))
    return center * lax.rsqrt(spread + EPS_LAYER) * gain_vec

def to_blocks(states):
    width_in = states.shape[-1]
    split_rows = states.reshape(N_DP, N_MP, BLOCKS, BLOCK // N_MP, width_in)
    return split_rows.transpose(0, 2, 1, 3, 4).reshape(N_DP * BLOCKS, BLOCK, width_in)

def encode(states, gain_vec, limits, weight):
    width_in = states.shape[-1]
    normed = layer_norm(to_blocks(states), gain_vec)
    keep_rows = (jnp.arange(BLOCK, dtype=jnp.int32)[None, :] < limits.reshape(-1)[:, None]).astype(jnp.float32)
    normed = (normed * keep_rows[:, :, None]).astype(jnp.bfloat16)
    projected = jnp.dot(normed.reshape(-1, width_in), weight, preferred_element_type=jnp.float32).astype(jnp.bfloat16)
    return projected.reshape(N_DP * BLOCKS, BLOCK, MODEL_WIDTH)

def reference(audio_states, image_states, audio_gain, image_gain, audio_proj, image_proj, block_rows, destination, input_gain, kv_weight):
    audio_tokens = encode(audio_states[0], audio_gain, block_rows[0], audio_proj)
    image_tokens = encode(image_states[1], image_gain, block_rows[1], image_proj)
    every_block = jnp.concatenate([audio_tokens, image_tokens], axis=0)
    flat_dest = destination.reshape(-1).astype(jnp.int32)
    hit_table = (flat_dest[:, None] == jnp.arange(2 * N_DP, dtype=jnp.int32)[None, :]).astype(jnp.int32)
    dest_rank = lax.optimization_barrier(jnp.sum((jnp.cumsum(hit_table, axis=0) - 1) * hit_table, axis=1))
    placement = (flat_dest * BLOCKS + dest_rank).astype(jnp.int32)
    gathered = jnp.zeros_like(every_block).at[placement].set(every_block)
    tokens = gathered.reshape(-1, MODEL_WIDTH).astype(jnp.float32)
    mean_square = lax.optimization_barrier(jnp.mean(tokens * tokens, axis=1))
    scaled = (tokens * input_gain).astype(jnp.bfloat16)
    projected_heads = jnp.dot(scaled, kv_weight, preferred_element_type=jnp.float32)
    key_values = (projected_heads * lax.rsqrt(mean_square + EPS_ROOT)[:, None]).astype(jnp.bfloat16)
    key_values = key_values.reshape(2, N_DP * BLOCKS * BLOCK, KV_WIDTH)
    backbone_rows = gathered.reshape(2, N_DP * BLOCKS * BLOCK, MODEL_WIDTH)
    key_values_full = jnp.concatenate([jnp.zeros_like(key_values), key_values], axis=0)
    rows_full = jnp.concatenate([jnp.zeros_like(backbone_rows), backbone_rows], axis=0)
    return (key_values_full, rows_full)
```

```python
import jax
import jax.numpy as jnp
from jax import lax
from jax.experimental import pallas as pl
from jax.experimental.pallas import tpu as pltpu
from jax.sharding import PartitionSpec as P

MESH = pl.DeviceIdType.MESH
BLOCK = 128
BLOCKS = 4
N_DP = 8
N_MP = 16
SHARE = BLOCK // N_MP
AW = 1280
IW = 3200
KW = AW + IW
FEAT = 512
KVC = 128
EPS_LAYER = 1e-05
EPS_ROOT = 1e-06
PART = 288

PARTS = (
    ((0, 0, 160, 0, 160, 0), (1, 0, 112, AW, 400, 160)),
    ((1, 112, 144, AW + 112, 400, 0), (1, 256, 144, AW + 256, 400, 144)),
)
COLS = ((0, 1536), (1536, 1536), (3072, 1408))


def remote(src, dst, ssem, rsem, dev):
    return pltpu.make_async_remote_copy(
        src_ref=src, dst_ref=dst, send_sem=ssem, recv_sem=rsem, device_id=dev, device_id_type=MESH
    )


def kernel(
    aud_ref, img_ref, again_ref, igain_ref, ap_ref, ip_ref, rows_ref, dest_ref, gin_ref, w_ref,
    kv_out, rows_out,
    abuf, ibuf, norm, aslot, islot, araw, iraw, ag, pbuf, cbuf, pown, wbuf, part, rtmp, ltmp, rbuf, lbuf, cfin,
    acc, kvacc, mssrc, msall,
    lsem, slot_s, aslot_r, islot_r, agr_s, agr_r, agl_s, agl_r, p_s, p_r, pf_s, pf_r,
    c_s, c_r, cf_s, cf_r, rr_s, rr_r, rl_s, rl_r, ms_s, ms_r,
):
    g = lax.axis_index("group")
    d = lax.axis_index("dp")
    m = lax.axis_index("mp")
    c = lax.rem(g, 2)
    y_hi = lax.div(d, 4)
    x = lax.rem(d, 4)
    right = lax.rem(m + 1, N_MP)
    left = lax.rem(m + N_MP - 1, N_MP)
    on_backbone = g >= 2

    barrier = pltpu.get_barrier_semaphore()

    @pl.loop(0, 32)
    def _(i):
        gg = lax.div(i, 8)
        dd = lax.rem(i, 8)

        @pl.when(i != g * 8 + d)
        def _():
            pl.semaphore_signal(barrier, inc=1, device_id=(gg, dd, m), device_id_type=MESH)

    pl.semaphore_signal(barrier, inc=1, device_id=(g, d, right), device_id_type=MESH)
    pl.semaphore_signal(barrier, inc=1, device_id=(g, d, left), device_id_type=MESH)

    def encoder(core, st_ref, buf, gain_ref, width, slot, raw, raw_sem):
        load = pltpu.make_async_copy(st_ref.at[0], buf, lsem.at[0])
        load.start()
        loadw = pltpu.make_async_copy(w_ref, wbuf, lsem.at[1])
        loadw.start()
        loads = []
        for j, (which, row, count, _, _, at) in enumerate(PARTS[core]):
            one = pltpu.make_async_copy(
                (ap_ref, ip_ref)[which].at[pl.ds(row, count)], pown.at[pl.ds(at, count)], lsem.at[2 + j]
            )
            one.start()
            loads.append(one)
        load.wait()
        gain = gain_ref[...].reshape(1, width)
        within = lax.broadcasted_iota(jnp.int32, (SHARE, 1), 0) + m * SHARE
        for b in range(BLOCKS):
            values = buf[pl.ds(b * SHARE, SHARE), :].astype(jnp.float32)
            center = values - jnp.mean(values, axis=-1, keepdims=True)
            spread = jnp.mean(center * center, axis=-1, keepdims=True)
            keep = jnp.where(within < rows_ref[core, d, b], 1.0, 0.0)
            norm[b, :, pl.ds(0, width)] = center * lax.rsqrt(spread + EPS_LAYER) * gain * keep

        @pl.loop(0, 2 * N_DP)
        def _(t):
            pick = jnp.int32(0)
            for b in range(BLOCKS):
                pick = jnp.where(dest_ref[core, d, b] == t, b, pick)
            slot[t] = norm[pick, :, pl.ds(0, width)].astype(jnp.bfloat16)

        pl.semaphore_wait(barrier, 33)

        def send_slot(t):
            return remote(
                slot.at[t], raw.at[d], slot_s.at[t], raw_sem.at[d], (2 + lax.div(t, N_DP), lax.rem(t, N_DP), m)
            )

        @pl.loop(0, 2 * N_DP)
        def _(t):
            send_slot(t).start()

        def send_part(x_to, j):
            which, row, count, base, per, _ = PARTS[core][j]
            return remote(
                (ap_ref, ip_ref)[which].at[pl.ds(row, count)],
                pbuf.at[pl.ds(pl.multiple_of(base + d * per, 16), count)],
                p_s.at[x_to, j], p_r.at[d, j], (2 + core, (1 - y_hi) * 4 + x_to, m),
            )

        for x_to in range(4):
            for j in range(2):
                send_part(x_to, j).start()

        for one in loads:
            one.wait()
        if core == 0:
            pown[pl.ds(272, 16), :] = jnp.zeros((16, FEAT), jnp.bfloat16)
        loadw.wait()
        pown[...] = (pown[...].astype(jnp.float32) * gin_ref[...].reshape(1, FEAT)).astype(jnp.bfloat16)

        @pl.loop(0, 8)
        def _(k):
            two = jnp.dot(
                pown[...], wbuf[:, pl.ds(pl.multiple_of(k * 256, 256), 256)], preferred_element_type=jnp.float32
            )
            part[2 * k] = two[:, :128]
            part[2 * k + 1] = two[:, 128:]

        def ring(s, tmp, buf, ssem, rsem, to):
            return remote(tmp.at[s], buf.at[s], ssem.at[s], rsem.at[s], (g, d, to))

        for s in range(9):
            if s < 8:
                mine = part[lax.rem(m + 8 - s, N_MP)]
                if s > 0:
                    ring(s - 1, rtmp, rbuf, rr_s, rr_r, right).wait_recv()
                    mine = mine + rbuf[s - 1].astype(jnp.float32)
                rtmp[s] = mine.astype(jnp.bfloat16)
                ring(s, rtmp, rbuf, rr_s, rr_r, right).start()
            if s < 7:
                mine = part[lax.rem(m + 9 + s, N_MP)]
                if s > 0:
                    ring(s - 1, ltmp, lbuf, rl_s, rl_r, left).wait_recv()
                    mine = mine + lbuf[s - 1].astype(jnp.float32)
                ltmp[s] = mine.astype(jnp.bfloat16)
                ring(s, ltmp, lbuf, rl_s, rl_r, left).start()
        ring(6, ltmp, lbuf, rl_s, rl_r, left).wait_recv()
        ring(7, rtmp, rbuf, rr_s, rr_r, right).wait_recv()
        cfin[...] = (part[m] + rbuf[7].astype(jnp.float32) + lbuf[6].astype(jnp.float32)).astype(jnp.bfloat16)

        def send_c(to, j):
            _, _, count, base, per, at = PARTS[core][j]
            return remote(
                cfin.at[pl.ds(at, count)], cbuf.at[pl.ds(pl.multiple_of(base + d * per, 16), count)],
                c_s.at[to, j], c_r.at[d, j], (2 + core, to, m),
            )

        for to in range(N_DP):
            for j in range(2):
                send_c(to, j).start()

        kv_out[...] = jnp.zeros_like(kv_out)
        rows_out[...] = jnp.zeros_like(rows_out)

        @pl.loop(0, 2 * N_DP)
        def _(t):
            send_slot(t).wait_send()

        for x_to in range(4):
            for j in range(2):
                send_part(x_to, j).wait_send()
        for s in range(8):
            ring(s, rtmp, rbuf, rr_s, rr_r, right).wait_send()
        for s in range(7):
            ring(s, ltmp, lbuf, rl_s, rl_r, left).wait_send()
        for to in range(N_DP):
            for j in range(2):
                send_c(to, j).wait_send()

    @pl.when(g == 0)
    def _():
        encoder(0, aud_ref, abuf, again_ref, AW, aslot, araw, aslot_r)

    @pl.when(g == 1)
    def _():
        encoder(1, img_ref, ibuf, igain_ref, IW, islot, iraw, islot_r)

    def backbone(core):
        me = core * N_DP + d
        own = []
        for k, (src, count, base) in enumerate(((ap_ref, 160, 0), (ip_ref, 400, AW))):
            one = pltpu.make_async_copy(
                src, pbuf.at[pl.ds(pl.multiple_of(base + d * count, 16), count)], lsem.at[k]
            )
            one.start()
            own.append(one)
        picks = []
        for s in range(2):
            found = jnp.int32(0)
            first = jnp.int32(0)
            second = jnp.int32(0)
            for e in range(N_DP):
                hit = dest_ref[s, e, 0] == me
                for b in range(1, BLOCKS):
                    hit = hit | (dest_ref[s, e, b] == me)
                first = jnp.where(hit & (found == 0), e, first)
                second = jnp.where(hit & (found == 1), e, second)
                found = found + jnp.where(hit, 1, 0)
            picks.append((first, second))
        pl.semaphore_wait(barrier, 33)

        for raw, sem in ((araw, aslot_r), (iraw, islot_r)):
            for e in range(N_DP):
                remote(raw.at[e], raw.at[e], slot_s.at[0], sem.at[e], (0, d, m)).wait_recv()
        for s, (raw, lo, width) in enumerate(((araw, 0, AW), (iraw, AW, IW))):
            both = jnp.concatenate(
                [raw[picks[s][0]].astype(jnp.float32), raw[picks[s][1]].astype(jnp.float32)], axis=0
            )
            ag[0, :, pl.ds(lo, width)] = both.astype(jnp.bfloat16)

        def go_right(s, p):
            cols = pl.ds(*COLS[p])
            return remote(
                ag.at[(16 - s) % 16, :, cols], ag.at[15 - s, :, cols], agr_s.at[s, p], agr_r.at[s, p], (g, d, right)
            )

        def go_left(s, p):
            cols = pl.ds(*COLS[p])
            return remote(ag.at[s, :, cols], ag.at[s + 1, :, cols], agl_s.at[s, p], agl_r.at[s, p], (g, d, left))

        def gather_step(s):
            for p in range(3):
                if s > 0:
                    go_right(s - 1, p).wait_recv()
                if s < 8:
                    go_right(s, p).start()
                if 0 < s < 8:
                    go_left(s - 1, p).wait_recv()
                if s < 7:
                    go_left(s, p).start()

        def send_part(k, j):
            which, row, count, base, per, _ = PARTS[core][j]
            return remote(
                (ap_ref, ip_ref)[which].at[pl.ds(row, count)],
                pbuf.at[pl.ds(pl.multiple_of(base + d * per, 16), count)],
                p_s.at[k, j], p_r.at[d, j], (2 + core, y_hi * 4 + lax.rem(x + k, 4), m),
            )

        def rows_of(e, core_of, j):
            _, _, count, base, per, _ = PARTS[core_of][j]
            return pl.ds(pl.multiple_of(base + e * per, 16), count)

        def forward(buf, e, core_of, j, ssem, rsem):
            rows = rows_of(e, core_of, j)
            return remote(buf.at[rows], buf.at[rows], ssem.at[e, j], rsem.at[e, j], (2 + (1 - core), d, m))

        def arrived(buf, e, j, rsem):
            rows = rows_of(e, core, j)
            remote(buf.at[rows], buf.at[rows], slot_s.at[0], rsem.at[e, j], (core, d, m)).wait_recv()

        def pass_on_p(e):
            for j in range(2):
                arrived(pbuf, e, j, p_r)
                forward(pbuf, e, core, j, pf_s, pf_r).start()

        gather_step(0)
        for k in range(1, 4):
            for j in range(2):
                send_part(k, j).start()
        for s in range(1, 5):
            gather_step(s)
        for k in range(1, 4):
            pass_on_p(y_hi * 4 + lax.rem(x + k, 4))
        for s in range(5, 8):
            gather_step(s)
        for k in range(4):
            pass_on_p((1 - y_hi) * 4 + k)
        gather_step(8)

        for one in own:
            one.wait()

        def others(body):
            for k in range(1, N_DP):
                body(lax.rem(d + k, N_DP))

        def take_p(e):
            for j in range(2):
                forward(pbuf, e, 1 - core, j, pf_s, pf_r).wait_recv()

        others(take_p)

        for s, (lo, width) in enumerate(((0, AW), (AW, IW))):
            @pl.loop(0, 2)
            def _(n):
                cols = pl.ds(pl.multiple_of(n * 256, 256), 256)
                acc[pl.ds(s * 256, 256), cols] = jnp.dot(
                    ag[:, :, pl.ds(lo, width)].reshape(256, width), pbuf[pl.ds(lo, width), cols],
                    preferred_element_type=jnp.float32,
                )

        for s in range(2):
            halves = []
            for r in range(2):
                tok = acc[pl.ds(s * 256 + r * 128, 128), :].astype(jnp.bfloat16).astype(jnp.float32)
                sq = tok * tok
                sq = sq[:, :128] + sq[:, 128:256] + sq[:, 256:384] + sq[:, 384:]
                halves.append(jnp.sum(sq.T, axis=0, keepdims=True))
            line = jnp.broadcast_to(jnp.concatenate(halves, axis=1), (8, 256))
            mssrc[:, pl.ds(s * 256, 256)] = pltpu.roll(line, m * 16, 1)[:1]

        def send_ms(k):
            return remote(
                mssrc, msall.at[k], ms_s.at[k], ms_r.at[k], (g, d, lax.rem(m + k, N_MP))
            )

        @pl.loop(1, N_MP)
        def _(k):
            send_ms(k).start()

        for e in range(N_DP):
            for j in range(2):
                arrived(cbuf, e, j, c_r)
                forward(cbuf, e, core, j, cf_s, cf_r).start()

        for s in range(2):
            for rel in range(16):
                z = lax.rem(m + rel, N_MP)
                for p in range(2):
                    rows_out[2 * s + p, z] = acc[pl.ds(s * 256 + rel * 16 + p * 8, 8), :].astype(jnp.bfloat16)

        for e in range(N_DP):
            for j in range(2):
                forward(cbuf, e, 1 - core, j, cf_s, cf_r).wait_recv()
        for s, (lo, width) in enumerate(((0, AW), (AW, IW))):
            kvacc[pl.ds(s * 256, 256), :] = jnp.dot(
                ag[:, :, pl.ds(lo, width)].reshape(256, width), cbuf[pl.ds(lo, width), :],
                preferred_element_type=jnp.float32,
            )

        @pl.loop(1, N_MP)
        def _(k):
            send_ms(k).wait_recv()

        total = mssrc[...]
        for k in range(1, N_MP):
            total = total + msall[k]
        scale = lax.rsqrt(total / (FEAT * N_MP) + EPS_ROOT)
        for s in range(2):
            line = jnp.broadcast_to(scale[:, s * 256 : s * 256 + 256], (8, 256))
            line = pltpu.roll(line, lax.rem((N_MP - m) * 16, 256), 1)
            for r in range(2):
                col = jnp.broadcast_to(line[:1, r * 128 : r * 128 + 128], (128, 128)).T
                at = pl.ds(s * 256 + r * 128, 128)
                kvacc[at, :] = kvacc[at, :] * col
        for s in range(2):
            for rel in range(16):
                z = lax.rem(m + rel, N_MP)
                for p in range(2):
                    kv_out[2 * s + p, z] = kvacc[pl.ds(s * 256 + rel * 16 + p * 8, 8), :].astype(jnp.bfloat16)

        for s in range(8):
            for p in range(3):
                go_right(s, p).wait_send()
                if s < 7:
                    go_left(s, p).wait_send()
        for k in range(1, 4):
            for j in range(2):
                send_part(k, j).wait_send()

        def sent(e):
            for j in range(2):
                forward(pbuf, e, core, j, pf_s, pf_r).wait_send()

        others(sent)
        for e in range(N_DP):
            for j in range(2):
                forward(cbuf, e, core, j, cf_s, cf_r).wait_send()

        @pl.loop(1, N_MP)
        def _(k):
            send_ms(k).wait_send()

    @pl.when(g == 2)
    def _():
        backbone(0)

    @pl.when(g == 3)
    def _():
        backbone(1)


def shards(
    audio_states, image_states, audio_gain, image_gain, audio_proj, image_proj,
    block_rows, destination, input_gain, kv_weight,
):
    anywhere = pl.BlockSpec(memory_space=pl.ANY)
    vmem = pl.BlockSpec(memory_space=pltpu.VMEM)
    smem = pl.BlockSpec(memory_space=pltpu.SMEM)
    bf, f32 = jnp.bfloat16, jnp.float32
    dma = pltpu.SemaphoreType.DMA
    kv, rows = pl.pallas_call(
        kernel,
        out_shape=(
            jax.ShapeDtypeStruct((BLOCKS, N_MP, SHARE, KVC), bf),
            jax.ShapeDtypeStruct((BLOCKS, N_MP, SHARE, FEAT), bf),
        ),
        in_specs=[anywhere, anywhere, vmem, vmem, anywhere, anywhere, smem, smem, vmem, anywhere],
        out_specs=(vmem, vmem),
        scratch_shapes=[
            pltpu.VMEM((32, AW), bf),
            pltpu.VMEM((32, IW), bf),
            pltpu.VMEM((BLOCKS, SHARE, IW), f32),
            pltpu.VMEM((2 * N_DP, SHARE, AW), bf),
            pltpu.VMEM((2 * N_DP, SHARE, IW), bf),
            pltpu.VMEM((N_DP, SHARE, AW), bf),
            pltpu.VMEM((N_DP, SHARE, IW), bf),
            pltpu.VMEM((N_MP, 16, KW), bf),
            pltpu.VMEM((KW, FEAT), bf),
            pltpu.VMEM((KW, KVC), bf),
            pltpu.VMEM((PART, FEAT), bf),
            pltpu.VMEM((FEAT, 2048), bf),
            pltpu.VMEM((N_MP, PART, KVC), f32),
            pltpu.VMEM((8, PART, KVC), bf),
            pltpu.VMEM((7, PART, KVC), bf),
            pltpu.VMEM((8, PART, KVC), bf),
            pltpu.VMEM((7, PART, KVC), bf),
            pltpu.VMEM((PART, KVC), bf),
            pltpu.VMEM((FEAT, FEAT), f32),
            pltpu.VMEM((FEAT, KVC), f32),
            pltpu.VMEM((1, FEAT), f32),
            pltpu.VMEM((N_MP, 1, FEAT), f32),
            dma((4,)),
            dma((16,)), dma((8,)), dma((8,)),
            dma((8, 3)), dma((8, 3)), dma((7, 3)), dma((7, 3)),
            dma((4, 2)), dma((8, 2)), dma((8, 2)), dma((8, 2)),
            dma((8, 2)), dma((8, 2)), dma((8, 2)), dma((8, 2)),
            dma((8,)), dma((8,)), dma((7,)), dma((7,)),
            dma((16,)), dma((16,)),
        ],
        compiler_params=pltpu.CompilerParams(
            collective_id=0, has_side_effects=True, vmem_limit_bytes=60 * 1024 * 1024
        ),
        name="route_project",
    )(
        audio_states, image_states, audio_gain, image_gain, audio_proj, image_proj,
        block_rows, destination, input_gain, kv_weight,
    )
    return (kv.reshape(1, BLOCKS * BLOCK, KVC), rows.reshape(1, BLOCKS * BLOCK, FEAT))


def solution(mesh):
    in_specs = (
        P("group", ("dp", "mp"), None),
        P("group", ("dp", "mp"), None),
        P(),
        P(),
        P("dp", "mp"),
        P("dp", "mp"),
        P(),
        P(),
        P("mp"),
        P("mp", None),
    )
    out_specs = (P("group", "dp", "mp"), P("group", "dp", "mp"))
    return jax.shard_map(shards, mesh=mesh, in_specs=in_specs, out_specs=out_specs, check_vma=False)
```

```python
import jax
import jax.numpy as jnp
from jax import lax
from jax.experimental import pallas as pl
from jax.experimental.pallas import tpu as pltpu
from jax.sharding import PartitionSpec as P

MESH = pl.DeviceIdType.MESH
BLOCK = 128
BLOCKS = 4
N_DP = 8
N_MP = 16
SHARE = BLOCK // N_MP
AW = 1280
IW = 3200
KW = AW + IW
FEAT = 512
KVC = 128
EPS_LAYER = 1e-05
EPS_ROOT = 1e-06
PART = 288
HALF = 144

PARTS = (
    ((0, 0, 160, 0, 160, 0), (1, 0, 112, AW, 400, 160)),
    ((1, 112, 144, AW + 112, 400, 0), (1, 256, 144, AW + 256, 400, 144)),
)
COLS = ((0, 1536), (1536, 1536), (3072, 1408))


def remote(src, dst, ssem, rsem, dev):
    return pltpu.make_async_remote_copy(
        src_ref=src, dst_ref=dst, send_sem=ssem, recv_sem=rsem, device_id=dev, device_id_type=MESH
    )


def kernel(
    aud_ref, img_ref, again_ref, igain_ref, ap_ref, ip_ref, rows_ref, dest_ref, gin_ref, w_ref,
    kv_out, rows_out,
    abuf, ibuf, norm, aslot, islot, araw, iraw, ag, pbuf, cbuf, pown, prel, wbuf, part, rtmp, ltmp, rbuf, lbuf, cfin,
    acc, kvacc, mssrc, msall,
    lsem, slot_s, aslot_r, islot_r, agr_s, agr_r, agl_s, agl_r, p_s, p_r, pf_s, pf_r,
    c_s, c_r, cf_s, cf_r, rr_s, rr_r, rl_s, rl_r, ms_s, ms_r, rel_s, rel_r,
):
    g = lax.axis_index("group")
    d = lax.axis_index("dp")
    m = lax.axis_index("mp")
    c = lax.rem(g, 2)
    y_hi = lax.div(d, 4)
    x = lax.rem(d, 4)
    right = lax.rem(m + 1, N_MP)
    left = lax.rem(m + N_MP - 1, N_MP)
    on_backbone = g >= 2

    barrier = pltpu.get_barrier_semaphore()

    @pl.loop(0, 32)
    def _(i):
        gg = lax.div(i, 8)
        dd = lax.rem(i, 8)

        @pl.when(i != g * 8 + d)
        def _():
            pl.semaphore_signal(barrier, inc=1, device_id=(gg, dd, m), device_id_type=MESH)

    pl.semaphore_signal(barrier, inc=1, device_id=(g, d, right), device_id_type=MESH)
    pl.semaphore_signal(barrier, inc=1, device_id=(g, d, left), device_id_type=MESH)

    def encoder(core, st_ref, buf, gain_ref, width, slot, raw, raw_sem):
        load = pltpu.make_async_copy(st_ref.at[0], buf, lsem.at[0])
        load.start()
        loadw = pltpu.make_async_copy(w_ref, wbuf, lsem.at[1])
        loadw.start()
        loads = []
        for j, (which, row, count, _, _, at) in enumerate(PARTS[core]):
            one = pltpu.make_async_copy(
                (ap_ref, ip_ref)[which].at[pl.ds(row, count)], pown.at[pl.ds(at, count)], lsem.at[2 + j]
            )
            one.start()
            loads.append(one)
        load.wait()
        gain = gain_ref[...].reshape(1, width)
        within = lax.broadcasted_iota(jnp.int32, (SHARE, 1), 0) + m * SHARE
        for b in range(BLOCKS):
            values = buf[pl.ds(b * SHARE, SHARE), :].astype(jnp.float32)
            center = values - jnp.mean(values, axis=-1, keepdims=True)
            spread = jnp.mean(center * center, axis=-1, keepdims=True)
            keep = jnp.where(within < rows_ref[core, b, d], 1.0, 0.0)
            norm[b, :, pl.ds(0, width)] = center * lax.rsqrt(spread + EPS_LAYER) * gain * keep

        @pl.loop(0, 2 * N_DP)
        def _(t):
            pick = jnp.int32(0)
            for b in range(BLOCKS):
                pick = jnp.where(dest_ref[core, b, d] == t, b, pick)
            slot[t] = norm[pick, :, pl.ds(0, width)].astype(jnp.bfloat16)

        pl.semaphore_wait(barrier, 33)

        def send_slot(t):
            return remote(
                slot.at[t], raw.at[d], slot_s.at[t], raw_sem.at[d], (2 + lax.div(t, N_DP), lax.rem(t, N_DP), m)
            )

        @pl.loop(0, N_DP)
        def _(t):
            send_slot(t).start()
            send_slot(t + N_DP).start()

        def send_part(x_to):
            which, row, count, base, per, _ = PARTS[core][0]
            return remote(
                (ap_ref, ip_ref)[which].at[pl.ds(row, count)],
                pbuf.at[pl.ds(pl.multiple_of(base + d * per, 16), count)],
                p_s.at[x_to, 0], p_r.at[d, 0], (2 + core, (1 - y_hi) * 4 + x_to, m),
            )

        count2, base2, per2 = PARTS[core][1][2:5]
        d_other = (1 - y_hi) * 4 + x

        def relay_part(x_to):
            return remote(
                prel.at[pl.ds(0, count2)],
                pbuf.at[pl.ds(pl.multiple_of(base2 + d_other * per2, 16), count2)],
                p_s.at[x_to, 1], p_r.at[d_other, 1], (2 + core, y_hi * 4 + x_to, m),
            )

        def send_parts():
            @pl.loop(0, 2 * N_DP)
            def _(t):
                send_slot(t).wait_send()

            for x_to in range(4):
                send_part(x_to).start()
            remote(
                prel.at[pl.ds(0, count2)], prel.at[pl.ds(0, count2)], rel_s.at[0], rel_r.at[0], (2 + core, d_other, m)
            ).wait_recv()
            for x_to in range(4):
                relay_part(x_to).start()

        for one in loads:
            one.wait()
        if core == 0:
            pown[pl.ds(272, 16), :] = jnp.zeros((16, FEAT), jnp.bfloat16)
        loadw.wait()
        pown[...] = (pown[...].astype(jnp.float32) * gin_ref[...].reshape(1, FEAT)).astype(jnp.bfloat16)

        @pl.loop(0, 8)
        def _(k):
            two = jnp.dot(
                pown[...], wbuf[:, pl.ds(pl.multiple_of(k * 256, 256), 256)], preferred_element_type=jnp.float32
            )
            part[2 * k] = two[:, :128]
            part[2 * k + 1] = two[:, 128:]

        def ring(s, h, tmp, buf, ssem, rsem, to):
            rows = pl.ds(h * HALF, HALF)
            return remote(tmp.at[s, rows], buf.at[s, rows], ssem.at[s, h], rsem.at[s, h], (g, d, to))

        def hop(s, h, chunk, tmp, buf, ssem, rsem, to):
            rows = pl.ds(h * HALF, HALF)
            mine = part[chunk, rows]
            if s > 0:
                ring(s - 1, h, tmp, buf, ssem, rsem, to).wait_recv()
                mine = mine + buf[s - 1, rows].astype(jnp.float32)
            tmp[s, rows] = mine.astype(jnp.bfloat16)
            ring(s, h, tmp, buf, ssem, rsem, to).start()

        for s in range(8):
            for h in range(2):
                hop(s, h, lax.rem(m + 8 - s, N_MP), rtmp, rbuf, rr_s, rr_r, right)
                if s < 7:
                    hop(s, h, lax.rem(m + 9 + s, N_MP), ltmp, lbuf, rl_s, rl_r, left)
            if s == 2:
                send_parts()
        for h in range(2):
            ring(6, h, ltmp, lbuf, rl_s, rl_r, left).wait_recv()
            ring(7, h, rtmp, rbuf, rr_s, rr_r, right).wait_recv()
        cfin[...] = (part[m] + rbuf[7].astype(jnp.float32) + lbuf[6].astype(jnp.float32)).astype(jnp.bfloat16)

        def send_c(to, j):
            _, _, count, base, per, at = PARTS[core][j]
            return remote(
                cfin.at[pl.ds(at, count)], cbuf.at[pl.ds(pl.multiple_of(base + d * per, 16), count)],
                c_s.at[to, j], c_r.at[d, j], (2 + core, to, m),
            )

        for to in range(N_DP):
            for j in range(2):
                send_c(to, j).start()

        kv_out[...] = jnp.zeros_like(kv_out)
        rows_out[...] = jnp.zeros_like(rows_out)

        for x_to in range(4):
            send_part(x_to).wait_send()
            relay_part(x_to).wait_send()
        for h in range(2):
            for s in range(8):
                ring(s, h, rtmp, rbuf, rr_s, rr_r, right).wait_send()
            for s in range(7):
                ring(s, h, ltmp, lbuf, rl_s, rl_r, left).wait_send()
        for to in range(N_DP):
            for j in range(2):
                send_c(to, j).wait_send()

    @pl.when(g == 0)
    def _():
        encoder(0, aud_ref, abuf, again_ref, AW, aslot, araw, aslot_r)

    @pl.when(g == 1)
    def _():
        encoder(1, img_ref, ibuf, igain_ref, IW, islot, iraw, islot_r)

    def backbone(core):
        me = core * N_DP + d
        own = []
        for k, (src, count, base) in enumerate(((ap_ref, 160, 0), (ip_ref, 400, AW))):
            one = pltpu.make_async_copy(
                src, pbuf.at[pl.ds(pl.multiple_of(base + d * count, 16), count)], lsem.at[k]
            )
            one.start()
            own.append(one)
        picks = []
        for s in range(2):
            found = jnp.int32(0)
            first = jnp.int32(0)
            second = jnp.int32(0)
            for e in range(N_DP):
                hit = dest_ref[s, 0, e] == me
                for b in range(1, BLOCKS):
                    hit = hit | (dest_ref[s, b, e] == me)
                first = jnp.where(hit & (found == 0), e, first)
                second = jnp.where(hit & (found == 1), e, second)
                found = found + jnp.where(hit, 1, 0)
            picks.append((first, second))
        pl.semaphore_wait(barrier, 33)

        which, row, count, _, _, _ = PARTS[core][1]
        to_relay = remote(
            (ap_ref, ip_ref)[which].at[pl.ds(row, count)], prel.at[pl.ds(0, count)], rel_s.at[0], rel_r.at[0],
            (core, (1 - y_hi) * 4 + x, m),
        )
        to_relay.start()

        for raw, sem in ((araw, aslot_r), (iraw, islot_r)):
            for e in range(N_DP):
                remote(raw.at[e], raw.at[e], slot_s.at[0], sem.at[e], (0, d, m)).wait_recv()
        for s, (raw, lo, width) in enumerate(((araw, 0, AW), (iraw, AW, IW))):
            both = jnp.concatenate(
                [raw[picks[s][0]].astype(jnp.float32), raw[picks[s][1]].astype(jnp.float32)], axis=0
            )
            ag[0, :, pl.ds(lo, width)] = both.astype(jnp.bfloat16)

        def go_right(s, p):
            cols = pl.ds(*COLS[p])
            return remote(
                ag.at[(16 - s) % 16, :, cols], ag.at[15 - s, :, cols], agr_s.at[s, p], agr_r.at[s, p], (g, d, right)
            )

        def go_left(s, p):
            cols = pl.ds(*COLS[p])
            return remote(ag.at[s, :, cols], ag.at[s + 1, :, cols], agl_s.at[s, p], agl_r.at[s, p], (g, d, left))

        def gather_step(s):
            for p in range(3):
                if s > 0:
                    go_right(s - 1, p).wait_recv()
                if s < 8:
                    go_right(s, p).start()
                if 0 < s < 8:
                    go_left(s - 1, p).wait_recv()
                if s < 7:
                    go_left(s, p).start()

        def send_part(k, j):
            which, row, count, base, per, _ = PARTS[core][j]
            return remote(
                (ap_ref, ip_ref)[which].at[pl.ds(row, count)],
                pbuf.at[pl.ds(pl.multiple_of(base + d * per, 16), count)],
                p_s.at[k, j], p_r.at[d, j], (2 + core, y_hi * 4 + lax.rem(x + k, 4), m),
            )

        def rows_of(e, core_of, j):
            _, _, count, base, per, _ = PARTS[core_of][j]
            return pl.ds(pl.multiple_of(base + e * per, 16), count)

        def forward(buf, e, core_of, j, ssem, rsem):
            rows = rows_of(e, core_of, j)
            return remote(buf.at[rows], buf.at[rows], ssem.at[e, j], rsem.at[e, j], (2 + (1 - core), d, m))

        def arrived(buf, e, j, rsem):
            rows = rows_of(e, core, j)
            remote(buf.at[rows], buf.at[rows], slot_s.at[0], rsem.at[e, j], (core, d, m)).wait_recv()

        def pass_on_p(e):
            for j in range(2):
                arrived(pbuf, e, j, p_r)
                forward(pbuf, e, core, j, pf_s, pf_r).start()

        gather_step(0)
        for k in range(1, 4):
            for j in range(2):
                send_part(k, j).start()
        for s in range(1, 7):
            gather_step(s)
        for k in range(1, 4):
            pass_on_p(y_hi * 4 + lax.rem(x + k, 4))
        gather_step(7)
        for k in range(4):
            pass_on_p((1 - y_hi) * 4 + k)
        gather_step(8)

        for one in own:
            one.wait()

        def others(body):
            for k in range(1, N_DP):
                body(lax.rem(d + k, N_DP))

        def take_p(e):
            for j in range(2):
                forward(pbuf, e, 1 - core, j, pf_s, pf_r).wait_recv()

        others(take_p)

        for s, (lo, width) in enumerate(((0, AW), (AW, IW))):
            @pl.loop(0, 2)
            def _(n):
                cols = pl.ds(pl.multiple_of(n * 256, 256), 256)
                acc[pl.ds(s * 256, 256), cols] = jnp.dot(
                    ag[:, :, pl.ds(lo, width)].reshape(256, width), pbuf[pl.ds(lo, width), cols],
                    preferred_element_type=jnp.float32,
                )

        for s in range(2):
            halves = []
            for r in range(2):
                tok = acc[pl.ds(s * 256 + r * 128, 128), :].astype(jnp.bfloat16).astype(jnp.float32)
                sq = tok * tok
                sq = sq[:, :128] + sq[:, 128:256] + sq[:, 256:384] + sq[:, 384:]
                halves.append(jnp.sum(sq.T, axis=0, keepdims=True))
            line = jnp.broadcast_to(jnp.concatenate(halves, axis=1), (8, 256))
            mssrc[:, pl.ds(s * 256, 256)] = pltpu.roll(line, m * 16, 1)[:1]

        def send_ms(k):
            return remote(
                mssrc, msall.at[k], ms_s.at[k], ms_r.at[k], (g, d, lax.rem(m + k, N_MP))
            )

        @pl.loop(1, N_MP)
        def _(k):
            send_ms(k).start()

        for e in range(N_DP):
            for j in range(2):
                arrived(cbuf, e, j, c_r)
                forward(cbuf, e, core, j, cf_s, cf_r).start()

        for s in range(2):
            for rel in range(16):
                z = lax.rem(m + rel, N_MP)
                for p in range(2):
                    rows_out[2 * s + p, z] = acc[pl.ds(s * 256 + rel * 16 + p * 8, 8), :].astype(jnp.bfloat16)

        for e in range(N_DP):
            for j in range(2):
                forward(cbuf, e, 1 - core, j, cf_s, cf_r).wait_recv()
        for s, (lo, width) in enumerate(((0, AW), (AW, IW))):
            kvacc[pl.ds(s * 256, 256), :] = jnp.dot(
                ag[:, :, pl.ds(lo, width)].reshape(256, width), cbuf[pl.ds(lo, width), :],
                preferred_element_type=jnp.float32,
            )

        @pl.loop(1, N_MP)
        def _(k):
            send_ms(k).wait_recv()

        total = mssrc[...]
        for k in range(1, N_MP):
            total = total + msall[k]
        scale = lax.rsqrt(total / (FEAT * N_MP) + EPS_ROOT)
        for s in range(2):
            line = jnp.broadcast_to(scale[:, s * 256 : s * 256 + 256], (8, 256))
            line = pltpu.roll(line, lax.rem((N_MP - m) * 16, 256), 1)
            for r in range(2):
                col = jnp.broadcast_to(line[:1, r * 128 : r * 128 + 128], (128, 128)).T
                at = pl.ds(s * 256 + r * 128, 128)
                kvacc[at, :] = kvacc[at, :] * col
        for s in range(2):
            for rel in range(16):
                z = lax.rem(m + rel, N_MP)
                for p in range(2):
                    kv_out[2 * s + p, z] = kvacc[pl.ds(s * 256 + rel * 16 + p * 8, 8), :].astype(jnp.bfloat16)

        to_relay.wait_send()
        for s in range(8):
            for p in range(3):
                go_right(s, p).wait_send()
                if s < 7:
                    go_left(s, p).wait_send()
        for k in range(1, 4):
            for j in range(2):
                send_part(k, j).wait_send()

        def sent(e):
            for j in range(2):
                forward(pbuf, e, core, j, pf_s, pf_r).wait_send()

        others(sent)
        for e in range(N_DP):
            for j in range(2):
                forward(cbuf, e, core, j, cf_s, cf_r).wait_send()

        @pl.loop(1, N_MP)
        def _(k):
            send_ms(k).wait_send()

    @pl.when(g == 2)
    def _():
        backbone(0)

    @pl.when(g == 3)
    def _():
        backbone(1)


def shards(
    audio_states, image_states, audio_gain, image_gain, audio_proj, image_proj,
    block_rows, destination, input_gain, kv_weight,
):
    anywhere = pl.BlockSpec(memory_space=pl.ANY)
    vmem = pl.BlockSpec(memory_space=pltpu.VMEM)
    smem = pl.BlockSpec(memory_space=pltpu.SMEM)
    bf, f32 = jnp.bfloat16, jnp.float32
    dma = pltpu.SemaphoreType.DMA
    kv, rows = pl.pallas_call(
        kernel,
        out_shape=(
            jax.ShapeDtypeStruct((BLOCKS, N_MP, SHARE, KVC), bf),
            jax.ShapeDtypeStruct((BLOCKS, N_MP, SHARE, FEAT), bf),
        ),
        in_specs=[anywhere, anywhere, vmem, vmem, anywhere, anywhere, smem, smem, vmem, anywhere],
        out_specs=(vmem, vmem),
        scratch_shapes=[
            pltpu.VMEM((32, AW), bf),
            pltpu.VMEM((32, IW), bf),
            pltpu.VMEM((BLOCKS, SHARE, IW), f32),
            pltpu.VMEM((2 * N_DP, SHARE, AW), bf),
            pltpu.VMEM((2 * N_DP, SHARE, IW), bf),
            pltpu.VMEM((N_DP, SHARE, AW), bf),
            pltpu.VMEM((N_DP, SHARE, IW), bf),
            pltpu.VMEM((N_MP, 16, KW), bf),
            pltpu.VMEM((KW, FEAT), bf),
            pltpu.VMEM((KW, KVC), bf),
            pltpu.VMEM((PART, FEAT), bf),
            pltpu.VMEM((160, FEAT), bf),
            pltpu.VMEM((FEAT, 2048), bf),
            pltpu.VMEM((N_MP, PART, KVC), f32),
            pltpu.VMEM((8, PART, KVC), bf),
            pltpu.VMEM((7, PART, KVC), bf),
            pltpu.VMEM((8, PART, KVC), bf),
            pltpu.VMEM((7, PART, KVC), bf),
            pltpu.VMEM((PART, KVC), bf),
            pltpu.VMEM((FEAT, FEAT), f32),
            pltpu.VMEM((FEAT, KVC), f32),
            pltpu.VMEM((1, FEAT), f32),
            pltpu.VMEM((N_MP, 1, FEAT), f32),
            dma((4,)),
            dma((16,)), dma((8,)), dma((8,)),
            dma((8, 3)), dma((8, 3)), dma((7, 3)), dma((7, 3)),
            dma((4, 2)), dma((8, 2)), dma((8, 2)), dma((8, 2)),
            dma((8, 2)), dma((8, 2)), dma((8, 2)), dma((8, 2)),
            dma((8, 2)), dma((8, 2)), dma((7, 2)), dma((7, 2)),
            dma((16,)), dma((16,)), dma((1,)), dma((1,)),
        ],
        compiler_params=pltpu.CompilerParams(
            collective_id=0, has_side_effects=True, vmem_limit_bytes=60 * 1024 * 1024
        ),
        name="route_project",
    )(
        audio_states, image_states, audio_gain, image_gain, audio_proj, image_proj,
        block_rows.transpose(0, 2, 1), destination.transpose(0, 2, 1), input_gain, kv_weight,
    )
    return (kv.reshape(1, BLOCKS * BLOCK, KVC), rows.reshape(1, BLOCKS * BLOCK, FEAT))


def solution(mesh):
    in_specs = (
        P("group", ("dp", "mp"), None),
        P("group", ("dp", "mp"), None),
        P(),
        P(),
        P("dp", "mp"),
        P("dp", "mp"),
        P(),
        P(),
        P("mp"),
        P("mp", None),
    )
    out_specs = (P("group", "dp", "mp"), P("group", "dp", "mp"))
    return jax.shard_map(shards, mesh=mesh, in_specs=in_specs, out_specs=out_specs, check_vma=False)
```

```python
import jax
import jax.numpy as jnp
from jax import lax
from jax.experimental import pallas as pl
from jax.experimental.pallas import tpu as pltpu
from jax.sharding import PartitionSpec as P

MESH = pl.DeviceIdType.MESH
BLOCK = 128
BLOCKS = 4
N_DP = 8
N_MP = 16
SHARE = BLOCK // N_MP
AW = 1280
IW = 3200
KW = AW + IW
FEAT = 512
KVC = 128
EPS_LAYER = 1e-05
EPS_ROOT = 1e-06
PART = 288
HALF = 144
GREETED = 22

PARTS = (
    ((0, 0, 160, 0, 160, 0), (1, 0, 112, AW, 400, 160)),
    ((1, 112, 144, AW + 112, 400, 0), (1, 256, 144, AW + 256, 400, 144)),
)
COLS = tuple((k * 896, 896) for k in range(5))
PIECES = len(COLS)
LAST_LEFT = 2


def remote(src, dst, ssem, rsem, dev):
    return pltpu.make_async_remote_copy(
        src_ref=src, dst_ref=dst, send_sem=ssem, recv_sem=rsem, device_id=dev, device_id_type=MESH
    )


def kernel(
    aud_ref, img_ref, again_hbm, igain_hbm, ap_ref, ip_ref, rows_hbm, dest_hbm, gin_hbm, w_ref,
    kv_out, rows_out,
    again_ref, igain_ref, gin_ref, rows_ref, dest_ref,
    abuf, ibuf, norm, aslot, islot, ahop, ihop, araw, iraw, ag, pbuf, cbuf, pown, prel, wbuf, part, rtmp, ltmp, rbuf, lbuf, cfin,
    acc, kvacc, mssrc, msall,
    lsem, slot_s, aslot_r, islot_r, agr_s, agr_r, agl_s, agl_r, p_s, p_r, pf_s, pf_r,
    c_s, c_r, cf_s, cf_r, rr_s, rr_r, rl_s, rl_r, ms_s, ms_r, rel_s, rel_r, sr_s, sr_r, so_s, tsem,
):
    g = lax.axis_index("group")
    d = lax.axis_index("dp")
    m = lax.axis_index("mp")
    c = lax.rem(g, 2)
    y_hi = lax.div(d, 4)
    x = lax.rem(d, 4)
    right = lax.rem(m + 1, N_MP)
    left = lax.rem(m + N_MP - 1, N_MP)
    on_backbone = g >= 2

    barrier = pltpu.get_barrier_semaphore()

    def greet(group, dp, mp):
        pl.semaphore_signal(barrier, inc=1, device_id=(group, dp, mp), device_id_type=MESH)

    tables = []
    for k, (src, dst) in enumerate(((dest_hbm, dest_ref), (rows_hbm, rows_ref))):
        one = pltpu.make_async_copy(src, dst, tsem.at[k])
        one.start()
        tables.append(one)

    @pl.loop(0, N_DP)
    def _(dd):
        greet(lax.rem(2 * lax.div(g, 2) + 2, 4), dd, m)
        greet(lax.rem(2 * lax.div(g, 2) + 2, 4) + 1, dd, m)

    for k in range(1, 4):
        greet(g, y_hi * 4 + lax.rem(x + k, 4), m)
    greet(2 * lax.div(g, 2) + 1 - c, d, m)
    greet(g, d, right)
    greet(g, d, left)

    def encoder(core, st_ref, buf, gain_hbm, gain_ref, width, slot, hopbuf, raw, raw_sem):
        load = pltpu.make_async_copy(st_ref.at[0], buf, lsem.at[0])
        load.start()
        loadg = pltpu.make_async_copy(gain_hbm, gain_ref, tsem.at[2])
        loadg.start()
        loadi = pltpu.make_async_copy(gin_hbm, gin_ref, tsem.at[3])
        loadi.start()
        loadw = pltpu.make_async_copy(w_ref, wbuf, lsem.at[1])
        loadw.start()
        loads = []
        for j, (which, row, count, _, _, at) in enumerate(PARTS[core]):
            one = pltpu.make_async_copy(
                (ap_ref, ip_ref)[which].at[pl.ds(row, count)], pown.at[pl.ds(at, count)], lsem.at[2 + j]
            )
            one.start()
            loads.append(one)
        load.wait()
        loadg.wait()
        for one in tables:
            one.wait()
        gain = gain_ref[...].reshape(1, width)
        within = lax.broadcasted_iota(jnp.int32, (SHARE, 1), 0) + m * SHARE
        for b in range(BLOCKS):
            values = buf[pl.ds(b * SHARE, SHARE), :].astype(jnp.float32)
            center = values - jnp.mean(values, axis=-1, keepdims=True)
            spread = jnp.mean(center * center, axis=-1, keepdims=True)
            keep = jnp.where(within < rows_ref[core, b, d], 1.0, 0.0)
            norm[b, :, pl.ds(0, width)] = center * lax.rsqrt(spread + EPS_LAYER) * gain * keep

        @pl.loop(0, 2 * N_DP)
        def _(t):
            pick = jnp.int32(0)
            for b in range(BLOCKS):
                pick = jnp.where(dest_ref[core, b, d] == t, b, pick)
            slot[t] = norm[pick, :, pl.ds(0, width)].astype(jnp.bfloat16)

        pl.semaphore_wait(barrier, GREETED)

        def send_slot(t):
            return remote(
                slot.at[t], raw.at[d], slot_s.at[t], raw_sem.at[d], (2 + lax.div(t, N_DP), lax.rem(t, N_DP), m)
            )

        far = y_hi * 4 + lax.rem(x + 2, 4)

        def slot_to_next(k):
            return remote(
                slot.at[k * N_DP + far], hopbuf.at[k], sr_s.at[k], sr_r.at[k], (core, y_hi * 4 + lax.rem(x + 1, 4), m)
            )

        def slot_onward(k):
            return remote(
                hopbuf.at[k], raw.at[y_hi * 4 + lax.rem(x + 3, 4)], so_s.at[k],
                raw_sem.at[y_hi * 4 + lax.rem(x + 3, 4)], (2 + k, y_hi * 4 + lax.rem(x + 1, 4), m),
            )

        for k in range(2):
            slot_to_next(k).start()

        @pl.loop(0, N_DP)
        def _(t):
            @pl.when(t != far)
            def _():
                send_slot(t).start()
                send_slot(t + N_DP).start()

        def send_part(x_to):
            which, row, count, base, per, _ = PARTS[core][0]
            return remote(
                (ap_ref, ip_ref)[which].at[pl.ds(row, count)],
                pbuf.at[pl.ds(pl.multiple_of(base + d * per, 16), count)],
                p_s.at[x_to, 0], p_r.at[d, 0], (2 + core, (1 - y_hi) * 4 + x_to, m),
            )

        count2, base2, per2 = PARTS[core][1][2:5]
        d_other = (1 - y_hi) * 4 + x

        def relay_part(x_to):
            return remote(
                prel.at[pl.ds(0, count2)],
                pbuf.at[pl.ds(pl.multiple_of(base2 + d_other * per2, 16), count2)],
                p_s.at[x_to, 1], p_r.at[d_other, 1], (2 + core, y_hi * 4 + x_to, m),
            )

        def send_parts():
            @pl.loop(0, N_DP)
            def _(t):
                @pl.when(t != far)
                def _():
                    send_slot(t).wait_send()
                    send_slot(t + N_DP).wait_send()

            for k in range(2):
                slot_onward(k).wait_send()

            for x_to in range(4):
                send_part(x_to).start()
            remote(
                prel.at[pl.ds(0, count2)], prel.at[pl.ds(0, count2)], rel_s.at[0], rel_r.at[0], (2 + core, d_other, m)
            ).wait_recv()
            for x_to in range(4):
                relay_part(x_to).start()

        for one in loads:
            one.wait()
        if core == 0:
            pown[pl.ds(272, 16), :] = jnp.zeros((16, FEAT), jnp.bfloat16)
        loadw.wait()
        loadi.wait()
        pown[...] = (pown[...].astype(jnp.float32) * gin_ref[...].reshape(1, FEAT)).astype(jnp.bfloat16)

        @pl.loop(0, 8)
        def _(k):
            two = jnp.dot(
                pown[...], wbuf[:, pl.ds(pl.multiple_of(k * 256, 256), 256)], preferred_element_type=jnp.float32
            )
            part[2 * k] = two[:, :128]
            part[2 * k + 1] = two[:, 128:]

        def ring(s, h, tmp, buf, ssem, rsem, to):
            rows = pl.ds(h * HALF, HALF)
            return remote(tmp.at[s, rows], buf.at[s, rows], ssem.at[s, h], rsem.at[s, h], (g, d, to))

        def hop(s, h, chunk, tmp, buf, ssem, rsem, to):
            rows = pl.ds(h * HALF, HALF)
            mine = part[chunk, rows]
            if s > 0:
                ring(s - 1, h, tmp, buf, ssem, rsem, to).wait_recv()
                mine = mine + buf[s - 1, rows].astype(jnp.float32)
            tmp[s, rows] = mine.astype(jnp.bfloat16)
            ring(s, h, tmp, buf, ssem, rsem, to).start()

        for k in range(2):
            slot_to_next(k).wait()
            slot_onward(k).start()
        for s in range(8):
            for h in range(2):
                hop(s, h, lax.rem(m + 8 - s, N_MP), rtmp, rbuf, rr_s, rr_r, right)
                if s < 7:
                    hop(s, h, lax.rem(m + 9 + s, N_MP), ltmp, lbuf, rl_s, rl_r, left)
            if s == 2:
                send_parts()
        for h in range(2):
            ring(6, h, ltmp, lbuf, rl_s, rl_r, left).wait_recv()
            ring(7, h, rtmp, rbuf, rr_s, rr_r, right).wait_recv()
        cfin[...] = (part[m] + rbuf[7].astype(jnp.float32) + lbuf[6].astype(jnp.float32)).astype(jnp.bfloat16)

        def send_c(to, j):
            _, _, count, base, per, at = PARTS[core][j]
            return remote(
                cfin.at[pl.ds(at, count)], cbuf.at[pl.ds(pl.multiple_of(base + d * per, 16), count)],
                c_s.at[to, j], c_r.at[d, j], (2 + core, to, m),
            )

        for to in range(N_DP):
            for j in range(2):
                send_c(to, j).start()

        kv_out[...] = jnp.zeros_like(kv_out)
        rows_out[...] = jnp.zeros_like(rows_out)

        for x_to in range(4):
            send_part(x_to).wait_send()
            relay_part(x_to).wait_send()
        for h in range(2):
            for s in range(8):
                ring(s, h, rtmp, rbuf, rr_s, rr_r, right).wait_send()
            for s in range(7):
                ring(s, h, ltmp, lbuf, rl_s, rl_r, left).wait_send()
        for to in range(N_DP):
            for j in range(2):
                send_c(to, j).wait_send()

    @pl.when(g == 0)
    def _():
        encoder(0, aud_ref, abuf, again_hbm, again_ref, AW, aslot, ahop, araw, aslot_r)

    @pl.when(g == 1)
    def _():
        encoder(1, img_ref, ibuf, igain_hbm, igain_ref, IW, islot, ihop, iraw, islot_r)

    def backbone(core):
        me = core * N_DP + d
        own = []
        for k, (src, count, base) in enumerate(((ap_ref, 160, 0), (ip_ref, 400, AW))):
            one = pltpu.make_async_copy(
                src, pbuf.at[pl.ds(pl.multiple_of(base + d * count, 16), count)], lsem.at[k]
            )
            one.start()
            own.append(one)
        for one in tables:
            one.wait()
        picks = []
        for s in range(2):
            found = jnp.int32(0)
            first = jnp.int32(0)
            second = jnp.int32(0)
            for e in range(N_DP):
                hit = dest_ref[s, 0, e] == me
                for b in range(1, BLOCKS):
                    hit = hit | (dest_ref[s, b, e] == me)
                first = jnp.where(hit & (found == 0), e, first)
                second = jnp.where(hit & (found == 1), e, second)
                found = found + jnp.where(hit, 1, 0)
            picks.append((first, second))
        pl.semaphore_wait(barrier, GREETED)

        which, row, count, _, _, _ = PARTS[core][1]
        to_relay = remote(
            (ap_ref, ip_ref)[which].at[pl.ds(row, count)], prel.at[pl.ds(0, count)], rel_s.at[0], rel_r.at[0],
            (core, (1 - y_hi) * 4 + x, m),
        )
        to_relay.start()

        for raw, sem in ((araw, aslot_r), (iraw, islot_r)):
            for e in range(N_DP):
                remote(raw.at[e], raw.at[e], slot_s.at[0], sem.at[e], (0, d, m)).wait_recv()
        for s, (raw, lo, width) in enumerate(((araw, 0, AW), (iraw, AW, IW))):
            both = jnp.concatenate(
                [raw[picks[s][0]].astype(jnp.float32), raw[picks[s][1]].astype(jnp.float32)], axis=0
            )
            ag[0, :, pl.ds(lo, width)] = both.astype(jnp.bfloat16)

        def go_right(s, p):
            cols = pl.ds(*COLS[p])
            return remote(
                ag.at[(16 - s) % 16, :, cols], ag.at[15 - s, :, cols], agr_s.at[s, p], agr_r.at[s, p], (g, d, right)
            )

        def go_left(s, p):
            cols = pl.ds(*COLS[p])
            return remote(ag.at[s, :, cols], ag.at[s + 1, :, cols], agl_s.at[s, p], agl_r.at[s, p], (g, d, left))

        def goes_right(s, p):
            return s < 7 or (s == 7 and p >= LAST_LEFT)

        def goes_left(s, p):
            return s < 7 or (s == 7 and p < LAST_LEFT)

        def gather_step(s):
            for p in range(PIECES):
                if s > 0 and goes_right(s - 1, p):
                    go_right(s - 1, p).wait_recv()
                if goes_right(s, p):
                    go_right(s, p).start()
                if s > 0 and goes_left(s - 1, p):
                    go_left(s - 1, p).wait_recv()
                if goes_left(s, p):
                    go_left(s, p).start()

        def send_part(k, j):
            which, row, count, base, per, _ = PARTS[core][j]
            return remote(
                (ap_ref, ip_ref)[which].at[pl.ds(row, count)],
                pbuf.at[pl.ds(pl.multiple_of(base + d * per, 16), count)],
                p_s.at[k, j], p_r.at[d, j], (2 + core, y_hi * 4 + lax.rem(x + k, 4), m),
            )

        def rows_of(e, core_of, j):
            _, _, count, base, per, _ = PARTS[core_of][j]
            return pl.ds(pl.multiple_of(base + e * per, 16), count)

        def forward(buf, e, core_of, j, ssem, rsem):
            rows = rows_of(e, core_of, j)
            return remote(buf.at[rows], buf.at[rows], ssem.at[e, j], rsem.at[e, j], (2 + (1 - core), d, m))

        def arrived(buf, e, j, rsem):
            rows = rows_of(e, core, j)
            remote(buf.at[rows], buf.at[rows], slot_s.at[0], rsem.at[e, j], (core, d, m)).wait_recv()

        def pass_on_p(e):
            for j in range(2):
                arrived(pbuf, e, j, p_r)
                forward(pbuf, e, core, j, pf_s, pf_r).start()

        gather_step(0)
        for k in range(1, 4):
            for j in range(2):
                send_part(k, j).start()
        for s in range(1, 7):
            gather_step(s)
        for k in range(1, 4):
            pass_on_p(y_hi * 4 + lax.rem(x + k, 4))
        gather_step(7)
        for k in range(4):
            pass_on_p((1 - y_hi) * 4 + k)
        gather_step(8)

        for one in own:
            one.wait()

        def others(body):
            for k in range(1, N_DP):
                body(lax.rem(d + k, N_DP))

        def take_p(e):
            for j in range(2):
                forward(pbuf, e, 1 - core, j, pf_s, pf_r).wait_recv()

        others(take_p)

        for s, (lo, width) in enumerate(((0, AW), (AW, IW))):
            @pl.loop(0, 2)
            def _(n):
                cols = pl.ds(pl.multiple_of(n * 256, 256), 256)
                acc[pl.ds(s * 256, 256), cols] = jnp.dot(
                    ag[:, :, pl.ds(lo, width)].reshape(256, width), pbuf[pl.ds(lo, width), cols],
                    preferred_element_type=jnp.float32,
                )

        for s in range(2):
            halves = []
            for r in range(2):
                tok = acc[pl.ds(s * 256 + r * 128, 128), :].astype(jnp.bfloat16).astype(jnp.float32)
                sq = tok * tok
                sq = sq[:, :128] + sq[:, 128:256] + sq[:, 256:384] + sq[:, 384:]
                halves.append(jnp.sum(sq.T, axis=0, keepdims=True))
            line = jnp.broadcast_to(jnp.concatenate(halves, axis=1), (8, 256))
            mssrc[:, pl.ds(s * 256, 256)] = pltpu.roll(line, m * 16, 1)[:1]

        def send_ms(k):
            return remote(
                mssrc, msall.at[k], ms_s.at[k], ms_r.at[k], (g, d, lax.rem(m + k, N_MP))
            )

        @pl.loop(1, N_MP)
        def _(k):
            send_ms(k).start()

        for e in range(N_DP):
            for j in range(2):
                arrived(cbuf, e, j, c_r)
                forward(cbuf, e, core, j, cf_s, cf_r).start()

        for s in range(2):
            for rel in range(16):
                z = lax.rem(m + rel, N_MP)
                for p in range(2):
                    rows_out[2 * s + p, z] = acc[pl.ds(s * 256 + rel * 16 + p * 8, 8), :].astype(jnp.bfloat16)

        for e in range(N_DP):
            for j in range(2):
                forward(cbuf, e, 1 - core, j, cf_s, cf_r).wait_recv()
        for s, (lo, width) in enumerate(((0, AW), (AW, IW))):
            kvacc[pl.ds(s * 256, 256), :] = jnp.dot(
                ag[:, :, pl.ds(lo, width)].reshape(256, width), cbuf[pl.ds(lo, width), :],
                preferred_element_type=jnp.float32,
            )

        to_relay.wait_send()
        for s in range(8):
            for p in range(PIECES):
                if goes_right(s, p):
                    go_right(s, p).wait_send()
                if goes_left(s, p):
                    go_left(s, p).wait_send()
        for k in range(1, 4):
            for j in range(2):
                send_part(k, j).wait_send()

        def sent(e):
            for j in range(2):
                forward(pbuf, e, core, j, pf_s, pf_r).wait_send()

        others(sent)
        for e in range(N_DP):
            for j in range(2):
                forward(cbuf, e, core, j, cf_s, cf_r).wait_send()

        @pl.loop(1, N_MP)
        def _(k):
            send_ms(k).wait_recv()

        total = mssrc[...]
        for k in range(1, N_MP):
            total = total + msall[k]
        scale = lax.rsqrt(total / (FEAT * N_MP) + EPS_ROOT)
        for s in range(2):
            line = jnp.broadcast_to(scale[:, s * 256 : s * 256 + 256], (8, 256))
            line = pltpu.roll(line, lax.rem((N_MP - m) * 16, 256), 1)
            for r in range(2):
                col = jnp.broadcast_to(line[:1, r * 128 : r * 128 + 128], (128, 128)).T
                at = pl.ds(s * 256 + r * 128, 128)
                kvacc[at, :] = kvacc[at, :] * col
        for s in range(2):
            for rel in range(16):
                z = lax.rem(m + rel, N_MP)
                for p in range(2):
                    kv_out[2 * s + p, z] = kvacc[pl.ds(s * 256 + rel * 16 + p * 8, 8), :].astype(jnp.bfloat16)

        @pl.loop(1, N_MP)
        def _(k):
            send_ms(k).wait_send()

    @pl.when(g == 2)
    def _():
        backbone(0)

    @pl.when(g == 3)
    def _():
        backbone(1)


def store(kv_in, rows_in, kv_out, rows_out, sem):
    one = pltpu.make_async_copy(rows_in, rows_out, sem.at[0])
    two = pltpu.make_async_copy(kv_in, kv_out, sem.at[1])
    one.start()
    two.start()
    one.wait()
    two.wait()


def shards(
    audio_states, image_states, audio_gain, image_gain, audio_proj, image_proj,
    block_rows, destination, input_gain, kv_weight,
):
    anywhere = pl.BlockSpec(memory_space=pl.ANY)
    vmem = pl.BlockSpec(memory_space=pltpu.VMEM)
    bf, f32 = jnp.bfloat16, jnp.float32
    dma = pltpu.SemaphoreType.DMA
    kv, rows = pl.pallas_call(
        kernel,
        out_shape=(
            pltpu.VMEM((BLOCKS, N_MP, SHARE, KVC), bf),
            pltpu.VMEM((BLOCKS, N_MP, SHARE, FEAT), bf),
        ),
        in_specs=[anywhere] * 10,
        out_specs=(vmem, vmem),
        scratch_shapes=[
            pltpu.VMEM((AW,), f32),
            pltpu.VMEM((IW,), f32),
            pltpu.VMEM((FEAT,), f32),
            pltpu.SMEM((2, BLOCKS, N_DP), jnp.int32),
            pltpu.SMEM((2, BLOCKS, N_DP), jnp.int32),
            pltpu.VMEM((32, AW), bf),
            pltpu.VMEM((32, IW), bf),
            pltpu.VMEM((BLOCKS, SHARE, IW), f32),
            pltpu.VMEM((2 * N_DP, SHARE, AW), bf),
            pltpu.VMEM((2 * N_DP, SHARE, IW), bf),
            pltpu.VMEM((2, SHARE, AW), bf),
            pltpu.VMEM((2, SHARE, IW), bf),
            pltpu.VMEM((N_DP, SHARE, AW), bf),
            pltpu.VMEM((N_DP, SHARE, IW), bf),
            pltpu.VMEM((N_MP, 16, KW), bf),
            pltpu.VMEM((KW, FEAT), bf),
            pltpu.VMEM((KW, KVC), bf),
            pltpu.VMEM((PART, FEAT), bf),
            pltpu.VMEM((160, FEAT), bf),
            pltpu.VMEM((FEAT, 2048), bf),
            pltpu.VMEM((N_MP, PART, KVC), f32),
            pltpu.VMEM((8, PART, KVC), bf),
            pltpu.VMEM((7, PART, KVC), bf),
            pltpu.VMEM((8, PART, KVC), bf),
            pltpu.VMEM((7, PART, KVC), bf),
            pltpu.VMEM((PART, KVC), bf),
            pltpu.VMEM((FEAT, FEAT), f32),
            pltpu.VMEM((FEAT, KVC), f32),
            pltpu.VMEM((1, FEAT), f32),
            pltpu.VMEM((N_MP, 1, FEAT), f32),
            dma((4,)),
            dma((16,)), dma((8,)), dma((8,)),
            dma((8, PIECES)), dma((8, PIECES)), dma((8, PIECES)), dma((8, PIECES)),
            dma((4, 2)), dma((8, 2)), dma((8, 2)), dma((8, 2)),
            dma((8, 2)), dma((8, 2)), dma((8, 2)), dma((8, 2)),
            dma((8, 2)), dma((8, 2)), dma((7, 2)), dma((7, 2)),
            dma((16,)), dma((16,)), dma((1,)), dma((1,)), dma((2,)), dma((2,)), dma((2,)), dma((4,)),
        ],
        compiler_params=pltpu.CompilerParams(
            collective_id=0, has_side_effects=True, vmem_limit_bytes=60 * 1024 * 1024
        ),
        name="route_project",
    )(
        audio_states, image_states, audio_gain, image_gain, audio_proj, image_proj,
        block_rows.transpose(0, 2, 1), destination.transpose(0, 2, 1), input_gain, kv_weight,
    )
    kv, rows = pl.pallas_call(
        store,
        out_shape=(
            jax.ShapeDtypeStruct((BLOCKS, N_MP, SHARE, KVC), bf),
            jax.ShapeDtypeStruct((BLOCKS, N_MP, SHARE, FEAT), bf),
        ),
        in_specs=[vmem, vmem],
        out_specs=(anywhere, anywhere),
        scratch_shapes=[dma((2,))],
        name="store",
    )(pltpu.with_memory_space_constraint(kv, pltpu.VMEM), pltpu.with_memory_space_constraint(rows, pltpu.VMEM))
    return (kv.reshape(1, BLOCKS * BLOCK, KVC), rows.reshape(1, BLOCKS * BLOCK, FEAT))


def solution(mesh):
    in_specs = (
        P("group", ("dp", "mp"), None),
        P("group", ("dp", "mp"), None),
        P(),
        P(),
        P("dp", "mp"),
        P("dp", "mp"),
        P(),
        P(),
        P("mp"),
        P("mp", None),
    )
    out_specs = (P("group", "dp", "mp"), P("group", "dp", "mp"))
    return jax.shard_map(shards, mesh=mesh, in_specs=in_specs, out_specs=out_specs, check_vma=False)
```

```python
import jax
import jax.numpy as jnp
from jax import lax
from jax.experimental import pallas as pl
from jax.experimental.pallas import tpu as pltpu
from jax.sharding import PartitionSpec as P

MESH = pl.DeviceIdType.MESH
BLOCK = 128
BLOCKS = 4
N_DP = 8
N_MP = 16
SHARE = BLOCK // N_MP
AW = 1280
IW = 3200
KW = AW + IW
FEAT = 512
KVC = 128
EPS_LAYER = 1e-05
EPS_ROOT = 1e-06
PART = 288
HALF = 144
GREETED = 22

PARTS = (
    ((0, 0, 160, 0, 160, 0), (1, 0, 112, AW, 400, 160)),
    ((1, 112, 144, AW + 112, 400, 0), (1, 256, 144, AW + 256, 400, 144)),
)
PART_ROWS = (272, 288)
COLS = ((0, 1280), (1280, 1152), (2432, 1024), (3456, 1024))
AUDIO_PIECES, IMAGE_PIECES = (0,), (1, 2, 3)
LAST_LEFT = 2


def remote(src, dst, ssem, rsem, dev):
    return pltpu.make_async_remote_copy(
        src_ref=src, dst_ref=dst, send_sem=ssem, recv_sem=rsem, device_id=dev, device_id_type=MESH
    )


def kernel(
    aud_ref, img_ref, again_hbm, igain_hbm, ap_ref, ip_ref, rows_hbm, dest_hbm, gin_hbm, w_ref,
    kv_out, rows_out,
    again_ref, igain_ref, gin_ref, rows_ref, dest_ref,
    abuf, ibuf, norm, aslot, islot, ahop, ihop, araw, iraw, ag, pbuf, cbuf, pown, prel, wbuf, part, rtmp, ltmp, rbuf, lbuf, cfin,
    acc, kvacc, mssrc, msall,
    lsem, slot_s, aslot_r, islot_r, ag_s, agr_r, agl_r, p_s, p_r, pf_s, pf_r,
    c_s, c_r, cf_s, cf_r, rr_s, rr_r, rl_s, rl_r, ms_s, ms_r, rel_s, rel_r, sr_s, sr_r, so_s, tsem,
):
    g = lax.axis_index("group")
    d = lax.axis_index("dp")
    m = lax.axis_index("mp")
    c = lax.rem(g, 2)
    y_hi = lax.div(d, 4)
    x = lax.rem(d, 4)
    right = lax.rem(m + 1, N_MP)
    left = lax.rem(m + N_MP - 1, N_MP)
    on_backbone = g >= 2

    barrier = pltpu.get_barrier_semaphore()

    def greet(group, dp, mp):
        pl.semaphore_signal(barrier, inc=1, device_id=(group, dp, mp), device_id_type=MESH)

    tables = []
    for k, (src, dst) in enumerate(((dest_hbm, dest_ref), (rows_hbm, rows_ref))):
        one = pltpu.make_async_copy(src, dst, tsem.at[k])
        one.start()
        tables.append(one)

    @pl.loop(0, N_DP)
    def _(dd):
        greet(lax.rem(2 * lax.div(g, 2) + 2, 4), dd, m)
        greet(lax.rem(2 * lax.div(g, 2) + 2, 4) + 1, dd, m)

    for k in range(1, 4):
        greet(g, y_hi * 4 + lax.rem(x + k, 4), m)
    greet(2 * lax.div(g, 2) + 1 - c, d, m)
    greet(g, d, right)
    greet(g, d, left)

    def encoder(core, st_ref, buf, gain_hbm, gain_ref, width, slot, hopbuf, raw, raw_sem):
        load = pltpu.make_async_copy(st_ref.at[0], buf, lsem.at[0])
        load.start()
        loadg = pltpu.make_async_copy(gain_hbm, gain_ref, tsem.at[2])
        loadg.start()
        loadi = pltpu.make_async_copy(gin_hbm, gin_ref, tsem.at[3])
        loadi.start()
        loadw = pltpu.make_async_copy(w_ref, wbuf, lsem.at[1])
        loadw.start()
        loads = []
        for j, (which, row, count, _, _, at) in enumerate(PARTS[core]):
            one = pltpu.make_async_copy(
                (ap_ref, ip_ref)[which].at[pl.ds(row, count)], pown.at[pl.ds(at, count)], lsem.at[2 + j]
            )
            one.start()
            loads.append(one)
        load.wait()
        loadg.wait()
        for one in tables:
            one.wait()
        gain = gain_ref[...].reshape(1, width)
        within = lax.broadcasted_iota(jnp.int32, (SHARE, 1), 0) + m * SHARE
        for b in range(BLOCKS):
            values = buf[pl.ds(b * SHARE, SHARE), :].astype(jnp.float32)
            center = values - jnp.mean(values, axis=-1, keepdims=True)
            spread = jnp.mean(center * center, axis=-1, keepdims=True)
            keep = jnp.where(within < rows_ref[core, b, d], 1.0, 0.0)
            norm[b, :, pl.ds(0, width)] = center * lax.rsqrt(spread + EPS_LAYER) * gain * keep

        @pl.loop(0, 2 * N_DP)
        def _(t):
            pick = jnp.int32(0)
            for b in range(BLOCKS):
                pick = jnp.where(dest_ref[core, b, d] == t, b, pick)
            slot[t] = norm[pick, :, pl.ds(0, width)].astype(jnp.bfloat16)

        pl.semaphore_wait(barrier, GREETED)

        def send_slot(t):
            return remote(
                slot.at[t], raw.at[d], slot_s.at[0], raw_sem.at[0], (2 + lax.div(t, N_DP), lax.rem(t, N_DP), m)
            )

        far = y_hi * 4 + lax.rem(x + 2, 4)

        def slot_to_next(k):
            return remote(
                slot.at[k * N_DP + far], hopbuf.at[k], sr_s.at[0], sr_r.at[0], (core, y_hi * 4 + lax.rem(x + 1, 4), m)
            )

        def slot_onward(k):
            return remote(
                hopbuf.at[k], raw.at[y_hi * 4 + lax.rem(x + 3, 4)], so_s.at[0], raw_sem.at[0],
                (2 + k, y_hi * 4 + lax.rem(x + 1, 4), m),
            )

        def both_hop(ssem, rsem):
            return remote(hopbuf, hopbuf, ssem.at[0], rsem.at[0], (core, y_hi * 4 + lax.rem(x + 1, 4), m))

        for k in range(2):
            slot_to_next(k).start()

        @pl.loop(0, N_DP)
        def _(t):
            @pl.when(t != far)
            def _():
                send_slot(t).start()
                send_slot(t + N_DP).start()

        def send_part(x_to):
            which, row, count, base, per, _ = PARTS[core][0]
            return remote(
                (ap_ref, ip_ref)[which].at[pl.ds(row, count)],
                pbuf.at[pl.ds(pl.multiple_of(base + d * per, 16), count)],
                p_s.at[0], p_r.at[d], (2 + core, (1 - y_hi) * 4 + x_to, m),
            )

        count2, base2, per2 = PARTS[core][1][2:5]
        d_other = (1 - y_hi) * 4 + x

        def relay_part(x_to):
            return remote(
                prel.at[pl.ds(0, count2)],
                pbuf.at[pl.ds(pl.multiple_of(base2 + d_other * per2, 16), count2)],
                p_s.at[0], p_r.at[d_other], (2 + core, y_hi * 4 + x_to, m),
            )

        def send_parts():
            remote(
                slot.at[pl.ds(0, 14)], slot.at[pl.ds(0, 14)], slot_s.at[0], raw_sem.at[0], (2, d, m)
            ).wait_send()
            both_hop(so_s, sr_r).wait_send()

            for x_to in range(4):
                send_part(x_to).start()
            remote(
                prel.at[pl.ds(0, count2)], prel.at[pl.ds(0, count2)], rel_s.at[0], rel_r.at[0], (2 + core, d_other, m)
            ).wait_recv()
            for x_to in range(4):
                relay_part(x_to).start()

        for one in loads:
            one.wait()
        if core == 0:
            pown[pl.ds(272, 16), :] = jnp.zeros((16, FEAT), jnp.bfloat16)
        loadw.wait()
        loadi.wait()
        pown[...] = (pown[...].astype(jnp.float32) * gin_ref[...].reshape(1, FEAT)).astype(jnp.bfloat16)

        @pl.loop(0, 8)
        def _(k):
            two = jnp.dot(
                pown[...], wbuf[:, pl.ds(pl.multiple_of(k * 256, 256), 256)], preferred_element_type=jnp.float32
            )
            part[2 * k] = two[:, :128]
            part[2 * k + 1] = two[:, 128:]

        def ring(s, h, tmp, buf, ssem, rsem, to):
            rows = pl.ds(h * HALF, HALF)
            return remote(tmp.at[s, rows], buf.at[s, rows], ssem.at[0], rsem.at[s, h], (g, d, to))

        def hop(s, h, chunk, tmp, buf, ssem, rsem, to):
            rows = pl.ds(h * HALF, HALF)
            mine = part[chunk, rows]
            if s > 0:
                ring(s - 1, h, tmp, buf, ssem, rsem, to).wait_recv()
                mine = mine + buf[s - 1, rows].astype(jnp.float32)
            tmp[s, rows] = mine.astype(jnp.bfloat16)
            ring(s, h, tmp, buf, ssem, rsem, to).start()

        both_hop(sr_s, sr_r).wait()
        for k in range(2):
            slot_onward(k).start()
        for s in range(8):
            for h in range(2):
                hop(s, h, lax.rem(m + 8 - s, N_MP), rtmp, rbuf, rr_s, rr_r, right)
                if s < 7:
                    hop(s, h, lax.rem(m + 9 + s, N_MP), ltmp, lbuf, rl_s, rl_r, left)
            if s == 2:
                send_parts()
        for h in range(2):
            ring(6, h, ltmp, lbuf, rl_s, rl_r, left).wait_recv()
            ring(7, h, rtmp, rbuf, rr_s, rr_r, right).wait_recv()
        cfin[...] = (part[m] + rbuf[7].astype(jnp.float32) + lbuf[6].astype(jnp.float32)).astype(jnp.bfloat16)

        def send_c(to, j):
            _, _, count, base, per, at = PARTS[core][j]
            return remote(
                cfin.at[pl.ds(at, count)], cbuf.at[pl.ds(pl.multiple_of(base + d * per, 16), count)],
                c_s.at[0], c_r.at[0], (2 + core, to, m),
            )

        for to in range(N_DP):
            for j in range(2):
                send_c(to, j).start()

        kv_out[...] = jnp.zeros_like(kv_out)
        rows_out[...] = jnp.zeros_like(rows_out)

        def all_sent(ref, rows, sem):
            remote(ref.at[pl.ds(0, rows)], ref.at[pl.ds(0, rows)], sem.at[0], c_r.at[0], (2 + core, d, m)).wait_send()

        all_sent(pbuf, 4 * PART_ROWS[core], p_s)
        all_sent(rtmp, 8, rr_s)
        all_sent(ltmp, 7, rl_s)
        all_sent(cbuf, N_DP * PART_ROWS[core], c_s)

    @pl.when(g == 0)
    def _():
        encoder(0, aud_ref, abuf, again_hbm, again_ref, AW, aslot, ahop, araw, aslot_r)

    @pl.when(g == 1)
    def _():
        encoder(1, img_ref, ibuf, igain_hbm, igain_ref, IW, islot, ihop, iraw, islot_r)

    def backbone(core):
        me = core * N_DP + d
        own = []
        for k, (src, count, base) in enumerate(((ap_ref, 160, 0), (ip_ref, 400, AW))):
            one = pltpu.make_async_copy(
                src, pbuf.at[pl.ds(pl.multiple_of(base + d * count, 16), count)], lsem.at[k]
            )
            one.start()
            own.append(one)
        for one in tables:
            one.wait()
        picks = []
        for s in range(2):
            found = jnp.int32(0)
            first = jnp.int32(0)
            second = jnp.int32(0)
            for e in range(N_DP):
                hit = dest_ref[s, 0, e] == me
                for b in range(1, BLOCKS):
                    hit = hit | (dest_ref[s, b, e] == me)
                first = jnp.where(hit & (found == 0), e, first)
                second = jnp.where(hit & (found == 1), e, second)
                found = found + jnp.where(hit, 1, 0)
            picks.append((first, second))
        pl.semaphore_wait(barrier, GREETED)

        which, row, count, _, _, _ = PARTS[core][1]
        to_relay = remote(
            (ap_ref, ip_ref)[which].at[pl.ds(row, count)], prel.at[pl.ds(0, count)], rel_s.at[0], rel_r.at[0],
            (core, (1 - y_hi) * 4 + x, m),
        )
        to_relay.start()

        def pick_rows(s, raw, sem, lo, width):
            remote(raw, raw, slot_s.at[0], sem.at[0], (0, d, m)).wait_recv()
            both = jnp.concatenate(
                [raw[picks[s][0]].astype(jnp.float32), raw[picks[s][1]].astype(jnp.float32)], axis=0
            )
            ag[0, :, pl.ds(lo, width)] = both.astype(jnp.bfloat16)

        def go_right(s, p):
            cols = pl.ds(*COLS[p])
            return remote(
                ag.at[(16 - s) % 16, :, cols], ag.at[15 - s, :, cols], ag_s.at[0], agr_r.at[s, p], (g, d, right)
            )

        def go_left(s, p):
            cols = pl.ds(*COLS[p])
            return remote(ag.at[s, :, cols], ag.at[s + 1, :, cols], ag_s.at[0], agl_r.at[s, p], (g, d, left))

        def goes_right(s, p):
            return s < 7 or (s == 7 and p >= LAST_LEFT)

        def goes_left(s, p):
            return s < 7 or (s == 7 and p < LAST_LEFT)

        def gather_step(s, pieces):
            for p in pieces:
                if s > 0 and goes_right(s - 1, p):
                    go_right(s - 1, p).wait_recv()
                if goes_right(s, p):
                    go_right(s, p).start()
                if s > 0 and goes_left(s - 1, p):
                    go_left(s - 1, p).wait_recv()
                if goes_left(s, p):
                    go_left(s, p).start()

        def send_part(k, j):
            which, row, count, base, per, _ = PARTS[core][j]
            return remote(
                (ap_ref, ip_ref)[which].at[pl.ds(row, count)],
                pbuf.at[pl.ds(pl.multiple_of(base + d * per, 16), count)],
                p_s.at[0], p_r.at[d], (2 + core, y_hi * 4 + lax.rem(x + k, 4), m),
            )

        def rows_of(e, core_of, j):
            _, _, count, base, per, _ = PARTS[core_of][j]
            return pl.ds(pl.multiple_of(base + e * per, 16), count)

        def forward(buf, e, core_of, j, ssem, rsem):
            rows = rows_of(e, core_of, j)
            return remote(buf.at[rows], buf.at[rows], ssem.at[0], rsem.at[0], (2 + (1 - core), d, m))

        def whole(buf, rows, ssem, rsem):
            return remote(buf.at[pl.ds(0, rows)], buf.at[pl.ds(0, rows)], ssem, rsem, (2 + (1 - core), d, m))

        def pass_on_p(e):
            whole(pbuf, PART_ROWS[core], p_s.at[0], p_r.at[e]).wait_recv()
            for j in range(2):
                forward(pbuf, e, core, j, pf_s, pf_r).start()

        pick_rows(0, araw, aslot_r, 0, AW)
        gather_step(0, AUDIO_PIECES)
        gather_step(1, AUDIO_PIECES)
        pick_rows(1, iraw, islot_r, AW, IW)
        gather_step(0, IMAGE_PIECES)
        for k in range(1, 4):
            for j in range(2):
                send_part(k, j).start()
        for s in range(1, 6):
            gather_step(s + 1, AUDIO_PIECES)
            gather_step(s, IMAGE_PIECES)
        for k in range(1, 4):
            pass_on_p(y_hi * 4 + lax.rem(x + k, 4))
        gather_step(7, AUDIO_PIECES)
        gather_step(6, IMAGE_PIECES)
        for k in range(4):
            pass_on_p((1 - y_hi) * 4 + k)
        gather_step(8, AUDIO_PIECES)
        gather_step(7, IMAGE_PIECES)

        for one in own:
            one.wait()

        whole(pbuf, 7 * PART_ROWS[1 - core], pf_s.at[0], pf_r.at[0]).wait_recv()

        def project(s, lo, width):
            @pl.loop(0, 2)
            def _(n):
                cols = pl.ds(pl.multiple_of(n * 256, 256), 256)
                acc[pl.ds(s * 256, 256), cols] = jnp.dot(
                    ag[:, :, pl.ds(lo, width)].reshape(256, width), pbuf[pl.ds(lo, width), cols],
                    preferred_element_type=jnp.float32,
                )

        project(0, 0, AW)
        gather_step(8, IMAGE_PIECES)
        project(1, AW, IW)

        for s in range(2):
            halves = []
            for r in range(2):
                tok = acc[pl.ds(s * 256 + r * 128, 128), :].astype(jnp.bfloat16).astype(jnp.float32)
                sq = tok * tok
                sq = sq[:, :128] + sq[:, 128:256] + sq[:, 256:384] + sq[:, 384:]
                halves.append(jnp.sum(sq.T, axis=0, keepdims=True))
            line = jnp.broadcast_to(jnp.concatenate(halves, axis=1), (8, 256))
            mssrc[:, pl.ds(s * 256, 256)] = pltpu.roll(line, m * 16, 1)[:1]

        def send_ms(k):
            return remote(
                mssrc, msall.at[k], ms_s.at[0], ms_r.at[0], (g, d, lax.rem(m + k, N_MP))
            )

        @pl.loop(1, N_MP)
        def _(k):
            send_ms(k).start()

        whole(cbuf, N_DP * PART_ROWS[core], c_s.at[0], c_r.at[0]).wait_recv()
        for e in range(N_DP):
            for j in range(2):
                forward(cbuf, e, core, j, cf_s, cf_r).start()

        for s in range(2):
            for rel in range(16):
                z = lax.rem(m + rel, N_MP)
                for p in range(2):
                    rows_out[2 * s + p, z] = acc[pl.ds(s * 256 + rel * 16 + p * 8, 8), :].astype(jnp.bfloat16)

        whole(cbuf, N_DP * PART_ROWS[1 - core], cf_s.at[0], cf_r.at[0]).wait_recv()
        for s, (lo, width) in enumerate(((0, AW), (AW, IW))):
            kvacc[pl.ds(s * 256, 256), :] = jnp.dot(
                ag[:, :, pl.ds(lo, width)].reshape(256, width), cbuf[pl.ds(lo, width), :],
                preferred_element_type=jnp.float32,
            )

        to_relay.wait_send()
        whole(ag, 15, ag_s.at[0], agr_r.at[0, 0]).wait_send()
        whole(pbuf, 3 * PART_ROWS[core], p_s.at[0], p_r.at[d]).wait_send()
        whole(pbuf, 7 * PART_ROWS[core], pf_s.at[0], pf_r.at[0]).wait_send()
        whole(cbuf, N_DP * PART_ROWS[core], cf_s.at[0], cf_r.at[0]).wait_send()

        all_ms = remote(
            msall.at[pl.ds(1, 15)], msall.at[pl.ds(1, 15)], ms_s.at[0], ms_r.at[0], (g, d, right)
        )
        all_ms.wait_recv()
        total = mssrc[...]
        for k in range(1, N_MP):
            total = total + msall[k]
        scale = lax.rsqrt(total / (FEAT * N_MP) + EPS_ROOT)
        for s in range(2):
            line = jnp.broadcast_to(scale[:, s * 256 : s * 256 + 256], (8, 256))
            line = pltpu.roll(line, lax.rem((N_MP - m) * 16, 256), 1)
            for r in range(2):
                col = jnp.broadcast_to(line[:1, r * 128 : r * 128 + 128], (128, 128)).T
                at = pl.ds(s * 256 + r * 128, 128)
                kvacc[at, :] = kvacc[at, :] * col
        for s in range(2):
            for rel in range(16):
                z = lax.rem(m + rel, N_MP)
                for p in range(2):
                    kv_out[2 * s + p, z] = kvacc[pl.ds(s * 256 + rel * 16 + p * 8, 8), :].astype(jnp.bfloat16)

        all_ms.wait_send()

    @pl.when(g == 2)
    def _():
        backbone(0)

    @pl.when(g == 3)
    def _():
        backbone(1)


def store(kv_in, rows_in, kv_out, rows_out, sem):
    one = pltpu.make_async_copy(rows_in, rows_out, sem.at[0])
    two = pltpu.make_async_copy(kv_in, kv_out, sem.at[1])
    one.start()
    two.start()
    one.wait()
    two.wait()


def shards(
    audio_states, image_states, audio_gain, image_gain, audio_proj, image_proj,
    block_rows, destination, input_gain, kv_weight,
):
    anywhere = pl.BlockSpec(memory_space=pl.ANY)
    vmem = pl.BlockSpec(memory_space=pltpu.VMEM)
    bf, f32 = jnp.bfloat16, jnp.float32
    dma = pltpu.SemaphoreType.DMA
    kv, rows = pl.pallas_call(
        kernel,
        out_shape=(
            pltpu.VMEM((BLOCKS, N_MP, SHARE, KVC), bf),
            pltpu.VMEM((BLOCKS, N_MP, SHARE, FEAT), bf),
        ),
        in_specs=[anywhere] * 10,
        out_specs=(vmem, vmem),
        scratch_shapes=[
            pltpu.VMEM((AW,), f32),
            pltpu.VMEM((IW,), f32),
            pltpu.VMEM((FEAT,), f32),
            pltpu.SMEM((2, BLOCKS, N_DP), jnp.int32),
            pltpu.SMEM((2, BLOCKS, N_DP), jnp.int32),
            pltpu.VMEM((32, AW), bf),
            pltpu.VMEM((32, IW), bf),
            pltpu.VMEM((BLOCKS, SHARE, IW), f32),
            pltpu.VMEM((2 * N_DP, SHARE, AW), bf),
            pltpu.VMEM((2 * N_DP, SHARE, IW), bf),
            pltpu.VMEM((2, SHARE, AW), bf),
            pltpu.VMEM((2, SHARE, IW), bf),
            pltpu.VMEM((N_DP, SHARE, AW), bf),
            pltpu.VMEM((N_DP, SHARE, IW), bf),
            pltpu.VMEM((N_MP, 16, KW), bf),
            pltpu.VMEM((KW, FEAT), bf),
            pltpu.VMEM((KW, KVC), bf),
            pltpu.VMEM((PART, FEAT), bf),
            pltpu.VMEM((160, FEAT), bf),
            pltpu.VMEM((FEAT, 2048), bf),
            pltpu.VMEM((N_MP, PART, KVC), f32),
            pltpu.VMEM((8, PART, KVC), bf),
            pltpu.VMEM((7, PART, KVC), bf),
            pltpu.VMEM((8, PART, KVC), bf),
            pltpu.VMEM((7, PART, KVC), bf),
            pltpu.VMEM((PART, KVC), bf),
            pltpu.VMEM((FEAT, FEAT), f32),
            pltpu.VMEM((FEAT, KVC), f32),
            pltpu.VMEM((1, FEAT), f32),
            pltpu.VMEM((N_MP, 1, FEAT), f32),
            dma((4,)),
            dma((1,)), dma((1,)), dma((1,)),
            dma((1,)), dma((8, 4)), dma((8, 4)),
            dma((1,)), dma((8,)), dma((1,)), dma((1,)),
            dma((1,)), dma((1,)), dma((1,)), dma((1,)),
            dma((1,)), dma((8, 2)), dma((1,)), dma((7, 2)),
            dma((1,)), dma((1,)), dma((1,)), dma((1,)), dma((1,)), dma((1,)), dma((1,)), dma((4,)),
        ],
        compiler_params=pltpu.CompilerParams(
            collective_id=0, has_side_effects=True, vmem_limit_bytes=60 * 1024 * 1024
        ),
        name="route_project",
    )(
        audio_states, image_states, audio_gain, image_gain, audio_proj, image_proj,
        block_rows.transpose(0, 2, 1), destination.transpose(0, 2, 1), input_gain, kv_weight,
    )
    kv, rows = pl.pallas_call(
        store,
        out_shape=(
            jax.ShapeDtypeStruct((BLOCKS, N_MP, SHARE, KVC), bf),
            jax.ShapeDtypeStruct((BLOCKS, N_MP, SHARE, FEAT), bf),
        ),
        in_specs=[vmem, vmem],
        out_specs=(anywhere, anywhere),
        scratch_shapes=[dma((2,))],
        name="store",
    )(pltpu.with_memory_space_constraint(kv, pltpu.VMEM), pltpu.with_memory_space_constraint(rows, pltpu.VMEM))
    return (kv.reshape(1, BLOCKS * BLOCK, KVC), rows.reshape(1, BLOCKS * BLOCK, FEAT))


def solution(mesh):
    in_specs = (
        P("group", ("dp", "mp"), None),
        P("group", ("dp", "mp"), None),
        P(),
        P(),
        P("dp", "mp"),
        P("dp", "mp"),
        P(),
        P(),
        P("mp"),
        P("mp", None),
    )
    out_specs = (P("group", "dp", "mp"), P("group", "dp", "mp"))
    return jax.shard_map(shards, mesh=mesh, in_specs=in_specs, out_specs=out_specs, check_vma=False)
```

```python
import jax
import jax.numpy as jnp
from jax import lax
from jax.experimental import pallas as pl
from jax.experimental.pallas import tpu as pltpu
from jax.sharding import PartitionSpec as P

MESH = pl.DeviceIdType.MESH
BLOCK = 128
BLOCKS = 4
N_DP = 8
N_MP = 16
SHARE = BLOCK // N_MP
AW = 1280
IW = 3200
KW = AW + IW
FEAT = 512
KVC = 128
EPS_LAYER = 1e-05
EPS_ROOT = 1e-06
PART = 288
HALF = 144
GREETED = 22

PARTS = (
    ((0, 0, 160, 0, 160, 0), (1, 0, 112, AW, 400, 160)),
    ((1, 112, 144, AW + 112, 400, 0), (1, 256, 144, AW + 256, 400, 144)),
)
PART_ROWS = (272, 288)
COLS = tuple((k * 640, 640) for k in range(7))
AUDIO_PIECES, IMAGE_PIECES = (0, 1), (2, 3, 4, 5, 6)
LAST_LEFT = 4


def remote(src, dst, ssem, rsem, dev):
    return pltpu.make_async_remote_copy(
        src_ref=src, dst_ref=dst, send_sem=ssem, recv_sem=rsem, device_id=dev, device_id_type=MESH
    )


def kernel(
    aud_ref, img_ref, again_hbm, igain_hbm, ap_ref, ip_ref, rows_hbm, dest_hbm, gin_hbm, w_ref,
    kv_out, rows_out,
    again_ref, igain_ref, gin_ref, rows_ref, dest_ref,
    abuf, ibuf, norm, aslot, islot, araw, iraw, ag, pbuf, cbuf, pown, prel, wbuf, part, rtmp, ltmp, rbuf, lbuf, cfin,
    acc, kvacc, mssrc, msall,
    lsem, slot_s, aslot_r, islot_r, ag_s, agr_r, agl_r, p_s, p_r, pf_s, pf_r,
    c_s, c_r, cf_s, cf_r, rr_s, rr_r, rl_s, rl_r, ms_s, ms_r, rel_s, rel_r, tsem,
):
    g = lax.axis_index("group")
    d = lax.axis_index("dp")
    m = lax.axis_index("mp")
    c = lax.rem(g, 2)
    y_hi = lax.div(d, 4)
    x = lax.rem(d, 4)
    right = lax.rem(m + 1, N_MP)
    left = lax.rem(m + N_MP - 1, N_MP)
    on_backbone = g >= 2

    barrier = pltpu.get_barrier_semaphore()

    def greet(group, dp, mp):
        pl.semaphore_signal(barrier, inc=1, device_id=(group, dp, mp), device_id_type=MESH)

    tables = []
    for k, (src, dst) in enumerate(((dest_hbm, dest_ref), (rows_hbm, rows_ref))):
        one = pltpu.make_async_copy(src, dst, tsem.at[k])
        one.start()
        tables.append(one)

    @pl.loop(0, N_DP)
    def _(dd):
        greet(lax.rem(2 * lax.div(g, 2) + 2, 4), dd, m)
        greet(lax.rem(2 * lax.div(g, 2) + 2, 4) + 1, dd, m)

    for k in range(1, 4):
        greet(g, y_hi * 4 + lax.rem(x + k, 4), m)
    greet(2 * lax.div(g, 2) + 1 - c, d, m)
    greet(g, d, right)
    greet(g, d, left)

    def encoder(core, st_ref, buf, gain_hbm, gain_ref, width, slot, raw, raw_sem):
        load = pltpu.make_async_copy(st_ref.at[0], buf, lsem.at[0])
        load.start()
        loadg = pltpu.make_async_copy(gain_hbm, gain_ref, tsem.at[2])
        loadg.start()
        loadi = pltpu.make_async_copy(gin_hbm, gin_ref, tsem.at[3])
        loadi.start()
        loadw = pltpu.make_async_copy(w_ref, wbuf, lsem.at[1])
        loadw.start()
        loads = []
        for j, (which, row, count, _, _, at) in enumerate(PARTS[core]):
            one = pltpu.make_async_copy(
                (ap_ref, ip_ref)[which].at[pl.ds(row, count)], pown.at[pl.ds(at, count)], lsem.at[2 + j]
            )
            one.start()
            loads.append(one)
        load.wait()
        loadg.wait()
        for one in tables:
            one.wait()
        gain = gain_ref[...].reshape(1, width)
        within = lax.broadcasted_iota(jnp.int32, (SHARE, 1), 0) + m * SHARE
        for b in range(BLOCKS):
            values = buf[pl.ds(b * SHARE, SHARE), :].astype(jnp.float32)
            center = values - jnp.mean(values, axis=-1, keepdims=True)
            spread = jnp.mean(center * center, axis=-1, keepdims=True)
            keep = jnp.where(within < rows_ref[core, b, d], 1.0, 0.0)
            norm[b, :, pl.ds(0, width)] = center * lax.rsqrt(spread + EPS_LAYER) * gain * keep

        @pl.loop(0, 2 * N_DP)
        def _(t):
            pick = jnp.int32(0)
            for b in range(BLOCKS):
                pick = jnp.where(dest_ref[core, b, d] == t, b, pick)
            slot[t] = norm[pick, :, pl.ds(0, width)].astype(jnp.bfloat16)

        pl.semaphore_wait(barrier, GREETED)

        def send_slot(t):
            return remote(
                slot.at[t], raw.at[d], slot_s.at[0], raw_sem.at[0], (2 + lax.div(t, N_DP), lax.rem(t, N_DP), m)
            )

        for k in (2, 1, 3, 0):
            for y in range(2):
                t = lax.rem(y_hi + y, 2) * 4 + lax.rem(x + k, 4)
                send_slot(t).start()
                send_slot(t + N_DP).start()

        def send_part(x_to):
            which, row, count, base, per, _ = PARTS[core][0]
            return remote(
                (ap_ref, ip_ref)[which].at[pl.ds(row, count)],
                pbuf.at[pl.ds(pl.multiple_of(base + d * per, 16), count)],
                p_s.at[0], p_r.at[d], (2 + core, (1 - y_hi) * 4 + x_to, m),
            )

        count2, base2, per2 = PARTS[core][1][2:5]
        d_other = (1 - y_hi) * 4 + x

        def relay_part(x_to):
            return remote(
                prel.at[pl.ds(0, count2)],
                pbuf.at[pl.ds(pl.multiple_of(base2 + d_other * per2, 16), count2)],
                p_s.at[0], p_r.at[d_other], (2 + core, y_hi * 4 + x_to, m),
            )

        def send_parts():
            remote(
                slot, slot, slot_s.at[0], raw_sem.at[0], (2, d, m)
            ).wait_send()

            for k in (2, 1, 3, 0):
                send_part(lax.rem(x + k, 4)).start()
            remote(
                prel.at[pl.ds(0, count2)], prel.at[pl.ds(0, count2)], rel_s.at[0], rel_r.at[0], (2 + core, d_other, m)
            ).wait_recv()
            for k in (2, 1, 3, 0):
                relay_part(lax.rem(x + k, 4)).start()

        for one in loads:
            one.wait()
        if core == 0:
            pown[pl.ds(272, 16), :] = jnp.zeros((16, FEAT), jnp.bfloat16)
        loadw.wait()
        loadi.wait()
        pown[...] = (pown[...].astype(jnp.float32) * gin_ref[...].reshape(1, FEAT)).astype(jnp.bfloat16)

        @pl.loop(0, 8)
        def _(k):
            two = jnp.dot(
                pown[...], wbuf[:, pl.ds(pl.multiple_of(k * 256, 256), 256)], preferred_element_type=jnp.float32
            )
            part[2 * k] = two[:, :128]
            part[2 * k + 1] = two[:, 128:]

        def ring(s, h, tmp, buf, ssem, rsem, to):
            rows = pl.ds(h * HALF, HALF)
            return remote(tmp.at[s, rows], buf.at[s, rows], ssem.at[0], rsem.at[s, h], (g, d, to))

        def hop(s, h, chunk, tmp, buf, ssem, rsem, to):
            rows = pl.ds(h * HALF, HALF)
            mine = part[chunk, rows]
            if s > 0:
                ring(s - 1, h, tmp, buf, ssem, rsem, to).wait_recv()
                mine = mine + buf[s - 1, rows].astype(jnp.float32)
            tmp[s, rows] = mine.astype(jnp.bfloat16)
            ring(s, h, tmp, buf, ssem, rsem, to).start()

        for s in range(8):
            for h in range(2):
                hop(s, h, lax.rem(m + 8 - s, N_MP), rtmp, rbuf, rr_s, rr_r, right)
                if s < 7:
                    hop(s, h, lax.rem(m + 9 + s, N_MP), ltmp, lbuf, rl_s, rl_r, left)
            if s == 2:
                send_parts()
        for h in range(2):
            ring(6, h, ltmp, lbuf, rl_s, rl_r, left).wait_recv()
            ring(7, h, rtmp, rbuf, rr_s, rr_r, right).wait_recv()
        cfin[...] = (part[m] + rbuf[7].astype(jnp.float32) + lbuf[6].astype(jnp.float32)).astype(jnp.bfloat16)

        def send_c(to, j):
            _, _, count, base, per, at = PARTS[core][j]
            return remote(
                cfin.at[pl.ds(at, count)], cbuf.at[pl.ds(pl.multiple_of(base + d * per, 16), count)],
                c_s.at[0], c_r.at[0], (2 + core, to, m),
            )

        for k in (2, 1, 3, 0):
            for y in range(2):
                for j in range(2):
                    send_c(lax.rem(y_hi + y, 2) * 4 + lax.rem(x + k, 4), j).start()

        kv_out[...] = jnp.zeros_like(kv_out)
        rows_out[...] = jnp.zeros_like(rows_out)

        def all_sent(ref, rows, sem):
            remote(ref.at[pl.ds(0, rows)], ref.at[pl.ds(0, rows)], sem.at[0], c_r.at[0], (2 + core, d, m)).wait_send()

        all_sent(pbuf, 4 * PART_ROWS[core], p_s)
        all_sent(rtmp, 8, rr_s)
        all_sent(ltmp, 7, rl_s)
        all_sent(cbuf, N_DP * PART_ROWS[core], c_s)

    @pl.when(g == 0)
    def _():
        encoder(0, aud_ref, abuf, again_hbm, again_ref, AW, aslot, araw, aslot_r)

    @pl.when(g == 1)
    def _():
        encoder(1, img_ref, ibuf, igain_hbm, igain_ref, IW, islot, iraw, islot_r)

    def backbone(core):
        me = core * N_DP + d
        own = []
        for k, (src, count, base) in enumerate(((ap_ref, 160, 0), (ip_ref, 400, AW))):
            one = pltpu.make_async_copy(
                src, pbuf.at[pl.ds(pl.multiple_of(base + d * count, 16), count)], lsem.at[k]
            )
            one.start()
            own.append(one)
        for one in tables:
            one.wait()
        picks = []
        for s in range(2):
            found = jnp.int32(0)
            first = jnp.int32(0)
            second = jnp.int32(0)
            for e in range(N_DP):
                hit = dest_ref[s, 0, e] == me
                for b in range(1, BLOCKS):
                    hit = hit | (dest_ref[s, b, e] == me)
                first = jnp.where(hit & (found == 0), e, first)
                second = jnp.where(hit & (found == 1), e, second)
                found = found + jnp.where(hit, 1, 0)
            picks.append((first, second))
        pl.semaphore_wait(barrier, GREETED)

        which, row, count, _, _, _ = PARTS[core][1]
        to_relay = remote(
            (ap_ref, ip_ref)[which].at[pl.ds(row, count)], prel.at[pl.ds(0, count)], rel_s.at[0], rel_r.at[0],
            (core, (1 - y_hi) * 4 + x, m),
        )
        to_relay.start()

        def pick_rows(s, raw, sem, lo, width):
            remote(raw, raw, slot_s.at[0], sem.at[0], (0, d, m)).wait_recv()
            both = jnp.concatenate(
                [raw[picks[s][0]].astype(jnp.float32), raw[picks[s][1]].astype(jnp.float32)], axis=0
            )
            ag[0, :, pl.ds(lo, width)] = both.astype(jnp.bfloat16)

        def go_right(s, p):
            cols = pl.ds(*COLS[p])
            return remote(
                ag.at[(16 - s) % 16, :, cols], ag.at[15 - s, :, cols], ag_s.at[0], agr_r.at[s, p], (g, d, right)
            )

        def go_left(s, p):
            cols = pl.ds(*COLS[p])
            return remote(ag.at[s, :, cols], ag.at[s + 1, :, cols], ag_s.at[0], agl_r.at[s, p], (g, d, left))

        def goes_right(s, p):
            return s < 7 or (s == 7 and p >= LAST_LEFT)

        def goes_left(s, p):
            return s < 7 or (s == 7 and p < LAST_LEFT)

        def gather_step(s, pieces):
            for p in pieces:
                if s > 0 and goes_right(s - 1, p):
                    go_right(s - 1, p).wait_recv()
                if goes_right(s, p):
                    go_right(s, p).start()
                if s > 0 and goes_left(s - 1, p):
                    go_left(s - 1, p).wait_recv()
                if goes_left(s, p):
                    go_left(s, p).start()

        def send_part(k, j):
            which, row, count, base, per, _ = PARTS[core][j]
            return remote(
                (ap_ref, ip_ref)[which].at[pl.ds(row, count)],
                pbuf.at[pl.ds(pl.multiple_of(base + d * per, 16), count)],
                p_s.at[0], p_r.at[d], (2 + core, y_hi * 4 + lax.rem(x + k, 4), m),
            )

        def rows_of(e, core_of, j):
            _, _, count, base, per, _ = PARTS[core_of][j]
            return pl.ds(pl.multiple_of(base + e * per, 16), count)

        def forward(buf, e, core_of, j, ssem, rsem):
            rows = rows_of(e, core_of, j)
            return remote(buf.at[rows], buf.at[rows], ssem.at[0], rsem.at[0], (2 + (1 - core), d, m))

        def whole(buf, rows, ssem, rsem):
            return remote(buf.at[pl.ds(0, rows)], buf.at[pl.ds(0, rows)], ssem, rsem, (2 + (1 - core), d, m))

        def pass_on_p(e):
            whole(pbuf, PART_ROWS[core], p_s.at[0], p_r.at[e]).wait_recv()
            for j in range(2):
                forward(pbuf, e, core, j, pf_s, pf_r).start()

        pick_rows(0, araw, aslot_r, 0, AW)
        gather_step(0, AUDIO_PIECES)
        pick_rows(1, iraw, islot_r, AW, IW)
        gather_step(0, IMAGE_PIECES)
        for k in range(1, 4):
            for j in range(2):
                send_part(k, j).start()
        for s in range(1, 6):
            gather_step(s, AUDIO_PIECES)
            gather_step(s, IMAGE_PIECES)
        for k in range(1, 4):
            pass_on_p(y_hi * 4 + lax.rem(x + k, 4))
        gather_step(6, AUDIO_PIECES)
        gather_step(6, IMAGE_PIECES)
        for k in range(4):
            pass_on_p((1 - y_hi) * 4 + k)
        gather_step(7, AUDIO_PIECES)
        gather_step(7, IMAGE_PIECES)
        gather_step(8, AUDIO_PIECES)

        for one in own:
            one.wait()

        whole(pbuf, 7 * PART_ROWS[1 - core], pf_s.at[0], pf_r.at[0]).wait_recv()

        def project(s, lo, width):
            @pl.loop(0, 2)
            def _(n):
                cols = pl.ds(pl.multiple_of(n * 256, 256), 256)
                acc[pl.ds(s * 256, 256), cols] = jnp.dot(
                    ag[:, :, pl.ds(lo, width)].reshape(256, width), pbuf[pl.ds(lo, width), cols],
                    preferred_element_type=jnp.float32,
                )

        project(0, 0, AW)
        gather_step(8, IMAGE_PIECES)
        project(1, AW, IW)

        for s in range(2):
            halves = []
            for r in range(2):
                tok = acc[pl.ds(s * 256 + r * 128, 128), :].astype(jnp.bfloat16).astype(jnp.float32)
                sq = tok * tok
                sq = sq[:, :128] + sq[:, 128:256] + sq[:, 256:384] + sq[:, 384:]
                halves.append(jnp.sum(sq.T, axis=0, keepdims=True))
            line = jnp.broadcast_to(jnp.concatenate(halves, axis=1), (8, 256))
            mssrc[:, pl.ds(s * 256, 256)] = pltpu.roll(line, m * 16, 1)[:1]

        def send_ms(k):
            return remote(
                mssrc, msall.at[k], ms_s.at[0], ms_r.at[0], (g, d, lax.rem(m + k, N_MP))
            )

        @pl.loop(1, N_MP)
        def _(k):
            send_ms(k).start()

        whole(cbuf, N_DP * PART_ROWS[core], c_s.at[0], c_r.at[0]).wait_recv()
        for e in range(N_DP):
            for j in range(2):
                forward(cbuf, e, core, j, cf_s, cf_r).start()

        for s in range(2):
            for rel in range(16):
                z = lax.rem(m + rel, N_MP)
                for p in range(2):
                    rows_out[2 * s + p, z] = acc[pl.ds(s * 256 + rel * 16 + p * 8, 8), :].astype(jnp.bfloat16)

        whole(cbuf, N_DP * PART_ROWS[1 - core], cf_s.at[0], cf_r.at[0]).wait_recv()
        for s, (lo, width) in enumerate(((0, AW), (AW, IW))):
            kvacc[pl.ds(s * 256, 256), :] = jnp.dot(
                ag[:, :, pl.ds(lo, width)].reshape(256, width), cbuf[pl.ds(lo, width), :],
                preferred_element_type=jnp.float32,
            )

        to_relay.wait_send()
        whole(ag, 15, ag_s.at[0], agr_r.at[0, 0]).wait_send()
        whole(pbuf, 3 * PART_ROWS[core], p_s.at[0], p_r.at[d]).wait_send()
        whole(pbuf, 7 * PART_ROWS[core], pf_s.at[0], pf_r.at[0]).wait_send()
        whole(cbuf, N_DP * PART_ROWS[core], cf_s.at[0], cf_r.at[0]).wait_send()

        all_ms = remote(
            msall.at[pl.ds(1, 15)], msall.at[pl.ds(1, 15)], ms_s.at[0], ms_r.at[0], (g, d, right)
        )
        all_ms.wait_recv()
        total = mssrc[...]
        for k in range(1, N_MP):
            total = total + msall[k]
        scale = lax.rsqrt(total / (FEAT * N_MP) + EPS_ROOT)
        for s in range(2):
            line = jnp.broadcast_to(scale[:, s * 256 : s * 256 + 256], (8, 256))
            line = pltpu.roll(line, lax.rem((N_MP - m) * 16, 256), 1)
            for r in range(2):
                col = jnp.broadcast_to(line[:1, r * 128 : r * 128 + 128], (128, 128)).T
                at = pl.ds(s * 256 + r * 128, 128)
                kvacc[at, :] = kvacc[at, :] * col
        for s in range(2):
            for rel in range(16):
                z = lax.rem(m + rel, N_MP)
                for p in range(2):
                    kv_out[2 * s + p, z] = kvacc[pl.ds(s * 256 + rel * 16 + p * 8, 8), :].astype(jnp.bfloat16)

        all_ms.wait_send()

    @pl.when(g == 2)
    def _():
        backbone(0)

    @pl.when(g == 3)
    def _():
        backbone(1)


def store(kv_in, rows_in, kv_out, rows_out, sem):
    one = pltpu.make_async_copy(rows_in, rows_out, sem.at[0])
    two = pltpu.make_async_copy(kv_in, kv_out, sem.at[1])
    one.start()
    two.start()
    one.wait()
    two.wait()


def shards(
    audio_states, image_states, audio_gain, image_gain, audio_proj, image_proj,
    block_rows, destination, input_gain, kv_weight,
):
    anywhere = pl.BlockSpec(memory_space=pl.ANY)
    vmem = pl.BlockSpec(memory_space=pltpu.VMEM)
    bf, f32 = jnp.bfloat16, jnp.float32
    dma = pltpu.SemaphoreType.DMA
    kv, rows = pl.pallas_call(
        kernel,
        out_shape=(
            pltpu.VMEM((BLOCKS, N_MP, SHARE, KVC), bf),
            pltpu.VMEM((BLOCKS, N_MP, SHARE, FEAT), bf),
        ),
        in_specs=[anywhere] * 10,
        out_specs=(vmem, vmem),
        scratch_shapes=[
            pltpu.VMEM((AW,), f32),
            pltpu.VMEM((IW,), f32),
            pltpu.VMEM((FEAT,), f32),
            pltpu.SMEM((2, BLOCKS, N_DP), jnp.int32),
            pltpu.SMEM((2, BLOCKS, N_DP), jnp.int32),
            pltpu.VMEM((32, AW), bf),
            pltpu.VMEM((32, IW), bf),
            pltpu.VMEM((BLOCKS, SHARE, IW), f32),
            pltpu.VMEM((2 * N_DP, SHARE, AW), bf),
            pltpu.VMEM((2 * N_DP, SHARE, IW), bf),
            pltpu.VMEM((N_DP, SHARE, AW), bf),
            pltpu.VMEM((N_DP, SHARE, IW), bf),
            pltpu.VMEM((N_MP, 16, KW), bf),
            pltpu.VMEM((KW, FEAT), bf),
            pltpu.VMEM((KW, KVC), bf),
            pltpu.VMEM((PART, FEAT), bf),
            pltpu.VMEM((160, FEAT), bf),
            pltpu.VMEM((FEAT, 2048), bf),
            pltpu.VMEM((N_MP, PART, KVC), f32),
            pltpu.VMEM((8, PART, KVC), bf),
            pltpu.VMEM((7, PART, KVC), bf),
            pltpu.VMEM((8, PART, KVC), bf),
            pltpu.VMEM((7, PART, KVC), bf),
            pltpu.VMEM((PART, KVC), bf),
            pltpu.VMEM((FEAT, FEAT), f32),
            pltpu.VMEM((FEAT, KVC), f32),
            pltpu.VMEM((1, FEAT), f32),
            pltpu.VMEM((N_MP, 1, FEAT), f32),
            dma((4,)),
            dma((1,)), dma((1,)), dma((1,)),
            dma((1,)), dma((8, 7)), dma((8, 7)),
            dma((1,)), dma((8,)), dma((1,)), dma((1,)),
            dma((1,)), dma((1,)), dma((1,)), dma((1,)),
            dma((1,)), dma((8, 2)), dma((1,)), dma((7, 2)),
            dma((1,)), dma((1,)), dma((1,)), dma((1,)), dma((4,)),
        ],
        compiler_params=pltpu.CompilerParams(
            collective_id=0, has_side_effects=True, vmem_limit_bytes=60 * 1024 * 1024
        ),
        name="route_project",
    )(
        audio_states, image_states, audio_gain, image_gain, audio_proj, image_proj,
        block_rows.transpose(0, 2, 1), destination.transpose(0, 2, 1), input_gain, kv_weight,
    )
    kv, rows = pl.pallas_call(
        store,
        out_shape=(
            jax.ShapeDtypeStruct((BLOCKS, N_MP, SHARE, KVC), bf),
            jax.ShapeDtypeStruct((BLOCKS, N_MP, SHARE, FEAT), bf),
        ),
        in_specs=[vmem, vmem],
        out_specs=(anywhere, anywhere),
        scratch_shapes=[dma((2,))],
        name="store",
    )(pltpu.with_memory_space_constraint(kv, pltpu.VMEM), pltpu.with_memory_space_constraint(rows, pltpu.VMEM))
    return (kv.reshape(1, BLOCKS * BLOCK, KVC), rows.reshape(1, BLOCKS * BLOCK, FEAT))


def solution(mesh):
    in_specs = (
        P("group", ("dp", "mp"), None),
        P("group", ("dp", "mp"), None),
        P(),
        P(),
        P("dp", "mp"),
        P("dp", "mp"),
        P(),
        P(),
        P("mp"),
        P("mp", None),
    )
    out_specs = (P("group", "dp", "mp"), P("group", "dp", "mp"))
    return jax.shard_map(shards, mesh=mesh, in_specs=in_specs, out_specs=out_specs, check_vma=False)
```

```python
import jax
import jax.numpy as jnp
from jax import lax
from jax.experimental import pallas as pl
from jax.experimental.pallas import tpu as pltpu
from jax.sharding import PartitionSpec as P

MESH = pl.DeviceIdType.MESH
BLOCK = 128
BLOCKS = 4
N_DP = 8
N_MP = 16
SHARE = BLOCK // N_MP
AW = 1280
IW = 3200
KW = AW + IW
FEAT = 512
KVC = 128
EPS_LAYER = 1e-05
EPS_ROOT = 1e-06
PART = 288
HALF = 144
GREETED = 22

PARTS = (
    ((0, 0, 160, 0, 160, 0), (1, 0, 112, AW, 400, 160)),
    ((1, 112, 144, AW + 112, 400, 0), (1, 256, 144, AW + 256, 400, 144)),
)
PART_ROWS = (272, 288)
COLS = tuple((k * 640, 640) for k in range(7))
AUDIO_PIECES, IMAGE_PIECES = (0, 1), (2, 3, 4, 5, 6)
LAST_LEFT = 4


def remote(src, dst, ssem, rsem, dev):
    return pltpu.make_async_remote_copy(
        src_ref=src, dst_ref=dst, send_sem=ssem, recv_sem=rsem, device_id=dev, device_id_type=MESH
    )


def kernel(
    aud_ref, img_ref, again_hbm, igain_hbm, ap_ref, ip_ref, rows_hbm, dest_hbm, gin_hbm, w_ref,
    kv_out, rows_out,
    again_ref, igain_ref, gin_ref, rows_ref, dest_ref,
    abuf, ibuf, norm, aslot, islot, araw, iraw, ag, pbuf, cbuf, pown, prel, wbuf, part, rtmp, ltmp, rbuf, lbuf, cfin,
    acc, kvacc, mssrc, msall,
    lsem, slot_s, aslot_r, islot_r, ag_s, agr_r, agl_r, p_s, p_r, pf_s, pf_r,
    c_s, c_r, cf_s, cf_r, rr_s, rr_r, rl_s, rl_r, ms_s, ms_r, rel_s, rel_r, tsem,
):
    g = lax.axis_index("group")
    d = lax.axis_index("dp")
    m = lax.axis_index("mp")
    c = lax.rem(g, 2)
    y_hi = lax.div(d, 4)
    x = lax.rem(d, 4)
    right = lax.rem(m + 1, N_MP)
    left = lax.rem(m + N_MP - 1, N_MP)
    on_backbone = g >= 2

    barrier = pltpu.get_barrier_semaphore()

    def greet(group, dp, mp):
        pl.semaphore_signal(barrier, inc=1, device_id=(group, dp, mp), device_id_type=MESH)

    tables = []
    for k, (src, dst) in enumerate(((dest_hbm, dest_ref), (rows_hbm, rows_ref))):
        one = pltpu.make_async_copy(src, dst, tsem.at[k])
        one.start()
        tables.append(one)

    @pl.loop(0, N_DP)
    def _(dd):
        greet(lax.rem(2 * lax.div(g, 2) + 2, 4), dd, m)
        greet(lax.rem(2 * lax.div(g, 2) + 2, 4) + 1, dd, m)

    for k in range(1, 4):
        greet(g, y_hi * 4 + lax.rem(x + k, 4), m)
    greet(2 * lax.div(g, 2) + 1 - c, d, m)
    greet(g, d, right)
    greet(g, d, left)

    def encoder(core, st_ref, buf, gain_hbm, gain_ref, width, slot, raw, raw_sem):
        load = pltpu.make_async_copy(st_ref.at[0], buf, lsem.at[0])
        load.start()
        loadg = pltpu.make_async_copy(gain_hbm, gain_ref, tsem.at[2])
        loadg.start()
        loadi = pltpu.make_async_copy(gin_hbm, gin_ref, tsem.at[3])
        loadi.start()
        loadw = pltpu.make_async_copy(w_ref, wbuf, lsem.at[1])
        loadw.start()
        loads = []
        for j, (which, row, count, _, _, at) in enumerate(PARTS[core]):
            one = pltpu.make_async_copy(
                (ap_ref, ip_ref)[which].at[pl.ds(row, count)], pown.at[pl.ds(at, count)], lsem.at[2 + j]
            )
            one.start()
            loads.append(one)
        load.wait()
        loadg.wait()
        for one in tables:
            one.wait()
        gain = gain_ref[...].reshape(1, width)
        within = lax.broadcasted_iota(jnp.int32, (SHARE, 1), 0) + m * SHARE
        for b in range(BLOCKS):
            values = buf[pl.ds(b * SHARE, SHARE), :].astype(jnp.float32)
            center = values - jnp.mean(values, axis=-1, keepdims=True)
            spread = jnp.mean(center * center, axis=-1, keepdims=True)
            keep = jnp.where(within < rows_ref[core, b, d], 1.0, 0.0)
            norm[b, :, pl.ds(0, width)] = center * lax.rsqrt(spread + EPS_LAYER) * gain * keep

        @pl.loop(0, 2 * N_DP)
        def _(t):
            pick = jnp.int32(0)
            for b in range(BLOCKS):
                pick = jnp.where(dest_ref[core, b, d] == t, b, pick)
            slot[t] = norm[pick, :, pl.ds(0, width)].astype(jnp.bfloat16)

        pl.semaphore_wait(barrier, GREETED)

        def send_slot(t):
            return remote(
                slot.at[t], raw.at[d], slot_s.at[0], raw_sem.at[0], (2 + lax.div(t, N_DP), lax.rem(t, N_DP), m)
            )

        for half in range(2):
            for k, y in ((2, 0), (1, 1), (3, 0), (0, 1), (2, 1), (1, 0), (3, 1), (0, 0)):
                t = lax.rem(y_hi + y, 2) * 4 + lax.rem(x + k, 4)
                send_slot(t + half * N_DP).start()

        def send_part(x_to):
            which, row, count, base, per, _ = PARTS[core][0]
            return remote(
                (ap_ref, ip_ref)[which].at[pl.ds(row, count)],
                pbuf.at[pl.ds(pl.multiple_of(base + d * per, 16), count)],
                p_s.at[0], p_r.at[d], (2 + core, (1 - y_hi) * 4 + x_to, m),
            )

        count2, base2, per2 = PARTS[core][1][2:5]
        d_other = (1 - y_hi) * 4 + x

        def relay_part(x_to):
            return remote(
                prel.at[pl.ds(0, count2)],
                pbuf.at[pl.ds(pl.multiple_of(base2 + d_other * per2, 16), count2)],
                p_s.at[0], p_r.at[d_other], (2 + core, y_hi * 4 + x_to, m),
            )

        def send_parts():
            remote(
                slot, slot, slot_s.at[0], raw_sem.at[0], (2, d, m)
            ).wait_send()

            for k in (2, 1, 3, 0):
                send_part(lax.rem(x + k, 4)).start()
            remote(
                prel.at[pl.ds(0, count2)], prel.at[pl.ds(0, count2)], rel_s.at[0], rel_r.at[0], (2 + core, d_other, m)
            ).wait_recv()
            for k in (2, 1, 3, 0):
                relay_part(lax.rem(x + k, 4)).start()

        for one in loads:
            one.wait()
        if core == 0:
            pown[pl.ds(272, 16), :] = jnp.zeros((16, FEAT), jnp.bfloat16)
        loadw.wait()
        loadi.wait()
        pown[...] = (pown[...].astype(jnp.float32) * gin_ref[...].reshape(1, FEAT)).astype(jnp.bfloat16)

        @pl.loop(0, 8)
        def _(k):
            two = jnp.dot(
                pown[...], wbuf[:, pl.ds(pl.multiple_of(k * 256, 256), 256)], preferred_element_type=jnp.float32
            )
            part[2 * k] = two[:, :128]
            part[2 * k + 1] = two[:, 128:]

        def ring(s, h, tmp, buf, ssem, rsem, to):
            rows = pl.ds(h * HALF, HALF)
            return remote(tmp.at[s, rows], buf.at[s, rows], ssem.at[0], rsem.at[s, h], (g, d, to))

        def hop(s, h, chunk, tmp, buf, ssem, rsem, to):
            rows = pl.ds(h * HALF, HALF)
            mine = part[chunk, rows]
            if s > 0:
                ring(s - 1, h, tmp, buf, ssem, rsem, to).wait_recv()
                mine = mine + buf[s - 1, rows].astype(jnp.float32)
            tmp[s, rows] = mine.astype(jnp.bfloat16)
            ring(s, h, tmp, buf, ssem, rsem, to).start()

        for s in range(8):
            for h in range(2):
                hop(s, h, lax.rem(m + 8 - s, N_MP), rtmp, rbuf, rr_s, rr_r, right)
                if s < 7:
                    hop(s, h, lax.rem(m + 9 + s, N_MP), ltmp, lbuf, rl_s, rl_r, left)
            if s == 2:
                send_parts()
        for h in range(2):
            ring(6, h, ltmp, lbuf, rl_s, rl_r, left).wait_recv()
            ring(7, h, rtmp, rbuf, rr_s, rr_r, right).wait_recv()
        cfin[...] = (part[m] + rbuf[7].astype(jnp.float32) + lbuf[6].astype(jnp.float32)).astype(jnp.bfloat16)

        def send_c(to, j):
            _, _, count, base, per, at = PARTS[core][j]
            return remote(
                cfin.at[pl.ds(at, count)], cbuf.at[pl.ds(pl.multiple_of(base + d * per, 16), count)],
                c_s.at[0], c_r.at[0], (2 + core, to, m),
            )

        for k in (2, 1, 3, 0):
            for y in range(2):
                for j in range(2):
                    send_c(lax.rem(y_hi + y, 2) * 4 + lax.rem(x + k, 4), j).start()

        kv_out[...] = jnp.zeros_like(kv_out)
        rows_out[...] = jnp.zeros_like(rows_out)

        def all_sent(ref, rows, sem):
            remote(ref.at[pl.ds(0, rows)], ref.at[pl.ds(0, rows)], sem.at[0], c_r.at[0], (2 + core, d, m)).wait_send()

        all_sent(pbuf, 4 * PART_ROWS[core], p_s)
        all_sent(rtmp, 8, rr_s)
        all_sent(ltmp, 7, rl_s)
        all_sent(cbuf, N_DP * PART_ROWS[core], c_s)

    @pl.when(g == 0)
    def _():
        encoder(0, aud_ref, abuf, again_hbm, again_ref, AW, aslot, araw, aslot_r)

    @pl.when(g == 1)
    def _():
        encoder(1, img_ref, ibuf, igain_hbm, igain_ref, IW, islot, iraw, islot_r)

    def backbone(core):
        me = core * N_DP + d
        own = []
        for k, (src, count, base) in enumerate(((ap_ref, 160, 0), (ip_ref, 400, AW))):
            one = pltpu.make_async_copy(
                src, pbuf.at[pl.ds(pl.multiple_of(base + d * count, 16), count)], lsem.at[k]
            )
            one.start()
            own.append(one)
        for one in tables:
            one.wait()
        picks = []
        for s in range(2):
            found = jnp.int32(0)
            first = jnp.int32(0)
            second = jnp.int32(0)
            for e in range(N_DP):
                hit = dest_ref[s, 0, e] == me
                for b in range(1, BLOCKS):
                    hit = hit | (dest_ref[s, b, e] == me)
                first = jnp.where(hit & (found == 0), e, first)
                second = jnp.where(hit & (found == 1), e, second)
                found = found + jnp.where(hit, 1, 0)
            picks.append((first, second))
        pl.semaphore_wait(barrier, GREETED)

        which, row, count, _, _, _ = PARTS[core][1]
        to_relay = remote(
            (ap_ref, ip_ref)[which].at[pl.ds(row, count)], prel.at[pl.ds(0, count)], rel_s.at[0], rel_r.at[0],
            (core, (1 - y_hi) * 4 + x, m),
        )
        to_relay.start()

        def pick_rows(s, raw, sem, lo, width):
            remote(raw, raw, slot_s.at[0], sem.at[0], (0, d, m)).wait_recv()
            both = jnp.concatenate(
                [raw[picks[s][0]].astype(jnp.float32), raw[picks[s][1]].astype(jnp.float32)], axis=0
            )
            ag[0, :, pl.ds(lo, width)] = both.astype(jnp.bfloat16)

        def go_right(s, p):
            cols = pl.ds(*COLS[p])
            return remote(
                ag.at[(16 - s) % 16, :, cols], ag.at[15 - s, :, cols], ag_s.at[0], agr_r.at[s, p], (g, d, right)
            )

        def go_left(s, p):
            cols = pl.ds(*COLS[p])
            return remote(ag.at[s, :, cols], ag.at[s + 1, :, cols], ag_s.at[0], agl_r.at[s, p], (g, d, left))

        def goes_right(s, p):
            return s < 7 or (s == 7 and p >= LAST_LEFT)

        def goes_left(s, p):
            return s < 7 or (s == 7 and p < LAST_LEFT)

        def gather_step(s, pieces):
            for p in pieces:
                if s > 0 and goes_right(s - 1, p):
                    go_right(s - 1, p).wait_recv()
                if goes_right(s, p):
                    go_right(s, p).start()
                if s > 0 and goes_left(s - 1, p):
                    go_left(s - 1, p).wait_recv()
                if goes_left(s, p):
                    go_left(s, p).start()

        def send_part(k, j):
            which, row, count, base, per, _ = PARTS[core][j]
            return remote(
                (ap_ref, ip_ref)[which].at[pl.ds(row, count)],
                pbuf.at[pl.ds(pl.multiple_of(base + d * per, 16), count)],
                p_s.at[0], p_r.at[d], (2 + core, y_hi * 4 + lax.rem(x + k, 4), m),
            )

        def rows_of(e, core_of, j):
            _, _, count, base, per, _ = PARTS[core_of][j]
            return pl.ds(pl.multiple_of(base + e * per, 16), count)

        def forward(buf, e, core_of, j, ssem, rsem):
            rows = rows_of(e, core_of, j)
            return remote(buf.at[rows], buf.at[rows], ssem.at[0], rsem.at[0], (2 + (1 - core), d, m))

        def whole(buf, rows, ssem, rsem):
            return remote(buf.at[pl.ds(0, rows)], buf.at[pl.ds(0, rows)], ssem, rsem, (2 + (1 - core), d, m))

        def pass_on_p(e):
            whole(pbuf, PART_ROWS[core], p_s.at[0], p_r.at[e]).wait_recv()
            for j in range(2):
                forward(pbuf, e, core, j, pf_s, pf_r).start()

        pick_rows(0, araw, aslot_r, 0, AW)
        gather_step(0, AUDIO_PIECES)
        pick_rows(1, iraw, islot_r, AW, IW)
        gather_step(0, IMAGE_PIECES)
        for k in range(1, 4):
            for j in range(2):
                send_part(k, j).start()
        for s in range(1, 6):
            gather_step(s, AUDIO_PIECES)
            gather_step(s, IMAGE_PIECES)
        for k in range(1, 4):
            pass_on_p(y_hi * 4 + lax.rem(x + k, 4))
        gather_step(6, AUDIO_PIECES)
        gather_step(6, IMAGE_PIECES)
        for k in range(4):
            pass_on_p((1 - y_hi) * 4 + k)
        gather_step(7, AUDIO_PIECES)
        gather_step(7, IMAGE_PIECES)
        gather_step(8, AUDIO_PIECES)

        for one in own:
            one.wait()

        whole(pbuf, 7 * PART_ROWS[1 - core], pf_s.at[0], pf_r.at[0]).wait_recv()

        def project(s, lo, width):
            @pl.loop(0, 2)
            def _(n):
                cols = pl.ds(pl.multiple_of(n * 256, 256), 256)
                acc[pl.ds(s * 256, 256), cols] = jnp.dot(
                    ag[:, :, pl.ds(lo, width)].reshape(256, width), pbuf[pl.ds(lo, width), cols],
                    preferred_element_type=jnp.float32,
                )

        project(0, 0, AW)
        gather_step(8, IMAGE_PIECES)
        project(1, AW, IW)

        for s in range(2):
            halves = []
            for r in range(2):
                tok = acc[pl.ds(s * 256 + r * 128, 128), :].astype(jnp.bfloat16).astype(jnp.float32)
                sq = tok * tok
                sq = sq[:, :128] + sq[:, 128:256] + sq[:, 256:384] + sq[:, 384:]
                halves.append(jnp.sum(sq.T, axis=0, keepdims=True))
            line = jnp.broadcast_to(jnp.concatenate(halves, axis=1), (8, 256))
            mssrc[:, pl.ds(s * 256, 256)] = pltpu.roll(line, m * 16, 1)[:1]

        def send_ms(k):
            return remote(
                mssrc, msall.at[k], ms_s.at[0], ms_r.at[0], (g, d, lax.rem(m + k, N_MP))
            )

        for k in (8, 7, 9, 6, 10, 5, 11, 4, 12, 3, 13, 2, 14, 1, 15):
            send_ms(k).start()

        whole(cbuf, N_DP * PART_ROWS[core], c_s.at[0], c_r.at[0]).wait_recv()
        for e in range(N_DP):
            for j in range(2):
                forward(cbuf, e, core, j, cf_s, cf_r).start()

        for s in range(2):
            for rel in range(16):
                z = lax.rem(m + rel, N_MP)
                for p in range(2):
                    rows_out[2 * s + p, z] = acc[pl.ds(s * 256 + rel * 16 + p * 8, 8), :].astype(jnp.bfloat16)

        whole(cbuf, N_DP * PART_ROWS[1 - core], cf_s.at[0], cf_r.at[0]).wait_recv()
        for s, (lo, width) in enumerate(((0, AW), (AW, IW))):
            kvacc[pl.ds(s * 256, 256), :] = jnp.dot(
                ag[:, :, pl.ds(lo, width)].reshape(256, width), cbuf[pl.ds(lo, width), :],
                preferred_element_type=jnp.float32,
            )

        to_relay.wait_send()
        whole(ag, 15, ag_s.at[0], agr_r.at[0, 0]).wait_send()
        whole(pbuf, 3 * PART_ROWS[core], p_s.at[0], p_r.at[d]).wait_send()
        whole(pbuf, 7 * PART_ROWS[core], pf_s.at[0], pf_r.at[0]).wait_send()
        whole(cbuf, N_DP * PART_ROWS[core], cf_s.at[0], cf_r.at[0]).wait_send()

        all_ms = remote(
            msall.at[pl.ds(1, 15)], msall.at[pl.ds(1, 15)], ms_s.at[0], ms_r.at[0], (g, d, right)
        )
        all_ms.wait_recv()
        total = mssrc[...]
        for k in range(1, N_MP):
            total = total + msall[k]
        scale = lax.rsqrt(total / (FEAT * N_MP) + EPS_ROOT)
        for s in range(2):
            line = jnp.broadcast_to(scale[:, s * 256 : s * 256 + 256], (8, 256))
            line = pltpu.roll(line, lax.rem((N_MP - m) * 16, 256), 1)
            for r in range(2):
                col = jnp.broadcast_to(line[:1, r * 128 : r * 128 + 128], (128, 128)).T
                at = pl.ds(s * 256 + r * 128, 128)
                kvacc[at, :] = kvacc[at, :] * col
        for s in range(2):
            for rel in range(16):
                z = lax.rem(m + rel, N_MP)
                for p in range(2):
                    kv_out[2 * s + p, z] = kvacc[pl.ds(s * 256 + rel * 16 + p * 8, 8), :].astype(jnp.bfloat16)

        all_ms.wait_send()

    @pl.when(g == 2)
    def _():
        backbone(0)

    @pl.when(g == 3)
    def _():
        backbone(1)


def store(kv_in, rows_in, kv_out, rows_out, sem):
    one = pltpu.make_async_copy(rows_in, rows_out, sem.at[0])
    two = pltpu.make_async_copy(kv_in, kv_out, sem.at[1])
    one.start()
    two.start()
    one.wait()
    two.wait()


def shards(
    audio_states, image_states, audio_gain, image_gain, audio_proj, image_proj,
    block_rows, destination, input_gain, kv_weight,
):
    anywhere = pl.BlockSpec(memory_space=pl.ANY)
    vmem = pl.BlockSpec(memory_space=pltpu.VMEM)
    bf, f32 = jnp.bfloat16, jnp.float32
    dma = pltpu.SemaphoreType.DMA
    kv, rows = pl.pallas_call(
        kernel,
        out_shape=(
            pltpu.VMEM((BLOCKS, N_MP, SHARE, KVC), bf),
            pltpu.VMEM((BLOCKS, N_MP, SHARE, FEAT), bf),
        ),
        in_specs=[anywhere] * 10,
        out_specs=(vmem, vmem),
        scratch_shapes=[
            pltpu.VMEM((AW,), f32),
            pltpu.VMEM((IW,), f32),
            pltpu.VMEM((FEAT,), f32),
            pltpu.SMEM((2, BLOCKS, N_DP), jnp.int32),
            pltpu.SMEM((2, BLOCKS, N_DP), jnp.int32),
            pltpu.VMEM((32, AW), bf),
            pltpu.VMEM((32, IW), bf),
            pltpu.VMEM((BLOCKS, SHARE, IW), f32),
            pltpu.VMEM((2 * N_DP, SHARE, AW), bf),
            pltpu.VMEM((2 * N_DP, SHARE, IW), bf),
            pltpu.VMEM((N_DP, SHARE, AW), bf),
            pltpu.VMEM((N_DP, SHARE, IW), bf),
            pltpu.VMEM((N_MP, 16, KW), bf),
            pltpu.VMEM((KW, FEAT), bf),
            pltpu.VMEM((KW, KVC), bf),
            pltpu.VMEM((PART, FEAT), bf),
            pltpu.VMEM((160, FEAT), bf),
            pltpu.VMEM((FEAT, 2048), bf),
            pltpu.VMEM((N_MP, PART, KVC), f32),
            pltpu.VMEM((8, PART, KVC), bf),
            pltpu.VMEM((7, PART, KVC), bf),
            pltpu.VMEM((8, PART, KVC), bf),
            pltpu.VMEM((7, PART, KVC), bf),
            pltpu.VMEM((PART, KVC), bf),
            pltpu.VMEM((FEAT, FEAT), f32),
            pltpu.VMEM((FEAT, KVC), f32),
            pltpu.VMEM((1, FEAT), f32),
            pltpu.VMEM((N_MP, 1, FEAT), f32),
            dma((4,)),
            dma((1,)), dma((1,)), dma((1,)),
            dma((1,)), dma((8, 7)), dma((8, 7)),
            dma((1,)), dma((8,)), dma((1,)), dma((1,)),
            dma((1,)), dma((1,)), dma((1,)), dma((1,)),
            dma((1,)), dma((8, 2)), dma((1,)), dma((7, 2)),
            dma((1,)), dma((1,)), dma((1,)), dma((1,)), dma((4,)),
        ],
        compiler_params=pltpu.CompilerParams(
            collective_id=0, has_side_effects=True, vmem_limit_bytes=60 * 1024 * 1024
        ),
        name="route_project",
    )(
        audio_states, image_states, audio_gain, image_gain, audio_proj, image_proj,
        block_rows.transpose(0, 2, 1), destination.transpose(0, 2, 1), input_gain, kv_weight,
    )
    kv, rows = pl.pallas_call(
        store,
        out_shape=(
            jax.ShapeDtypeStruct((BLOCKS, N_MP, SHARE, KVC), bf),
            jax.ShapeDtypeStruct((BLOCKS, N_MP, SHARE, FEAT), bf),
        ),
        in_specs=[vmem, vmem],
        out_specs=(anywhere, anywhere),
        scratch_shapes=[dma((2,))],
        name="store",
    )(pltpu.with_memory_space_constraint(kv, pltpu.VMEM), pltpu.with_memory_space_constraint(rows, pltpu.VMEM))
    return (kv.reshape(1, BLOCKS * BLOCK, KVC), rows.reshape(1, BLOCKS * BLOCK, FEAT))


def solution(mesh):
    in_specs = (
        P("group", ("dp", "mp"), None),
        P("group", ("dp", "mp"), None),
        P(),
        P(),
        P("dp", "mp"),
        P("dp", "mp"),
        P(),
        P(),
        P("mp"),
        P("mp", None),
    )
    out_specs = (P("group", "dp", "mp"), P("group", "dp", "mp"))
    return jax.shard_map(shards, mesh=mesh, in_specs=in_specs, out_specs=out_specs, check_vma=False)
```

```python
import jax
import jax.numpy as jnp
from jax import lax
from jax.experimental import pallas as pl
from jax.experimental.pallas import tpu as pltpu
from jax.sharding import PartitionSpec as P

MESH = pl.DeviceIdType.MESH
BLOCK = 128
BLOCKS = 4
N_DP = 8
N_MP = 16
SHARE = BLOCK // N_MP
AW = 1280
IW = 3200
KW = AW + IW
FEAT = 512
KVC = 128
EPS_LAYER = 1e-05
EPS_ROOT = 1e-06
PART = 288
HALF = 144
GREETED = 22

PARTS = (
    ((0, 0, 160, 0, 160, 0), (1, 0, 112, AW, 400, 160)),
    ((1, 112, 144, AW + 112, 400, 0), (1, 256, 144, AW + 256, 400, 144)),
)
PART_ROWS = (272, 288)
COLS = tuple((k * 640, 640) for k in range(7))
AUDIO_PIECES, IMAGE_PIECES = (0, 1), (2, 3, 4, 5, 6)
LAST_LEFT = 4


def remote(src, dst, ssem, rsem, dev):
    return pltpu.make_async_remote_copy(
        src_ref=src, dst_ref=dst, send_sem=ssem, recv_sem=rsem, device_id=dev, device_id_type=MESH
    )


def kernel(
    aud_ref, img_ref, again_hbm, igain_hbm, ap_ref, ip_ref, rows_hbm, dest_hbm, gin_hbm, w_ref,
    kv_out, rows_out,
    again_ref, igain_ref, gin_ref, rows_ref, dest_ref,
    abuf, ibuf, norm, aslot, islot, araw, iraw, ag, pbuf, cbuf, pown, prel, wbuf, part, rtmp, ltmp, rbuf, lbuf, cfin,
    acc, kvacc, mssrc, msall,
    lsem, slot_s, aslot_r, islot_r, ag_s, agr_r, agl_r, p_s, p_r, pf_s, pf_r,
    c_s, c_r, cf_s, cf_r, rr_s, rr_r, rl_s, rl_r, ms_s, ms_r, rel_s, rel_r, tsem,
):
    g = lax.axis_index("group")
    d = lax.axis_index("dp")
    m = lax.axis_index("mp")
    c = lax.rem(g, 2)
    y_hi = lax.div(d, 4)
    x = lax.rem(d, 4)
    right = lax.rem(m + 1, N_MP)
    left = lax.rem(m + N_MP - 1, N_MP)
    on_backbone = g >= 2

    barrier = pltpu.get_barrier_semaphore()

    def greet(group, dp, mp):
        pl.semaphore_signal(barrier, inc=1, device_id=(group, dp, mp), device_id_type=MESH)

    tables = []
    for k, (src, dst) in enumerate(((dest_hbm, dest_ref), (rows_hbm, rows_ref))):
        one = pltpu.make_async_copy(src, dst, tsem.at[k])
        one.start()
        tables.append(one)

    @pl.loop(0, N_DP)
    def _(dd):
        greet(lax.rem(2 * lax.div(g, 2) + 2, 4), dd, m)
        greet(lax.rem(2 * lax.div(g, 2) + 2, 4) + 1, dd, m)

    for k in range(1, 4):
        greet(g, y_hi * 4 + lax.rem(x + k, 4), m)
    greet(2 * lax.div(g, 2) + 1 - c, d, m)
    greet(g, d, right)
    greet(g, d, left)

    def encoder(core, st_ref, buf, gain_hbm, gain_ref, width, slot, raw, raw_sem):
        load = pltpu.make_async_copy(st_ref.at[0], buf, lsem.at[0])
        load.start()
        loadg = pltpu.make_async_copy(gain_hbm, gain_ref, tsem.at[2])
        loadg.start()
        loadi = pltpu.make_async_copy(gin_hbm, gin_ref, tsem.at[3])
        loadi.start()
        loadw = pltpu.make_async_copy(w_ref, wbuf, lsem.at[1])
        loadw.start()
        loads = []
        for j, (which, row, count, _, _, at) in enumerate(PARTS[core]):
            one = pltpu.make_async_copy(
                (ap_ref, ip_ref)[which].at[pl.ds(row, count)], pown.at[pl.ds(at, count)], lsem.at[2 + j]
            )
            one.start()
            loads.append(one)
        load.wait()
        loadg.wait()
        for one in tables:
            one.wait()
        gain = gain_ref[...].reshape(1, width)
        within = lax.broadcasted_iota(jnp.int32, (SHARE, 1), 0) + m * SHARE
        for b in range(BLOCKS):
            values = buf[pl.ds(b * SHARE, SHARE), :].astype(jnp.float32)
            center = values - jnp.mean(values, axis=-1, keepdims=True)
            spread = jnp.mean(center * center, axis=-1, keepdims=True)
            keep = jnp.where(within < rows_ref[core, b, d], 1.0, 0.0)
            norm[b, :, pl.ds(0, width)] = center * lax.rsqrt(spread + EPS_LAYER) * gain * keep

        @pl.loop(0, 2 * N_DP)
        def _(t):
            pick = jnp.int32(0)
            for b in range(BLOCKS):
                pick = jnp.where(dest_ref[core, b, d] == t, b, pick)
            slot[t] = norm[pick, :, pl.ds(0, width)].astype(jnp.bfloat16)

        pl.semaphore_wait(barrier, GREETED)

        def send_slot(t):
            return remote(
                slot.at[t], raw.at[d], slot_s.at[0], raw_sem.at[0], (2 + lax.div(t, N_DP), lax.rem(t, N_DP), m)
            )

        for half in range(2):
            for k, y in ((2, 0), (0, 1), (1, 0), (3, 1), (0, 0), (2, 1), (1, 1), (3, 0)):
                t = lax.rem(y_hi + y, 2) * 4 + lax.rem(x + k, 4)
                send_slot(t + half * N_DP).start()

        def send_part(x_to):
            which, row, count, base, per, _ = PARTS[core][0]
            return remote(
                (ap_ref, ip_ref)[which].at[pl.ds(row, count)],
                pbuf.at[pl.ds(pl.multiple_of(base + d * per, 16), count)],
                p_s.at[0], p_r.at[d], (2 + core, (1 - y_hi) * 4 + x_to, m),
            )

        count2, base2, per2 = PARTS[core][1][2:5]
        d_other = (1 - y_hi) * 4 + x

        def relay_part(x_to):
            return remote(
                prel.at[pl.ds(0, count2)],
                pbuf.at[pl.ds(pl.multiple_of(base2 + d_other * per2, 16), count2)],
                p_s.at[0], p_r.at[d_other], (2 + core, y_hi * 4 + x_to, m),
            )

        def send_parts():
            remote(
                slot, slot, slot_s.at[0], raw_sem.at[0], (2, d, m)
            ).wait_send()

            for k in (2, 1, 3, 0):
                send_part(lax.rem(x + k, 4)).start()
            remote(
                prel.at[pl.ds(0, count2)], prel.at[pl.ds(0, count2)], rel_s.at[0], rel_r.at[0], (2 + core, d_other, m)
            ).wait_recv()
            for k in (2, 1, 3, 0):
                relay_part(lax.rem(x + k, 4)).start()

        for one in loads:
            one.wait()
        if core == 0:
            pown[pl.ds(272, 16), :] = jnp.zeros((16, FEAT), jnp.bfloat16)
        loadw.wait()
        loadi.wait()
        pown[...] = (pown[...].astype(jnp.float32) * gin_ref[...].reshape(1, FEAT)).astype(jnp.bfloat16)

        @pl.loop(0, 8)
        def _(k):
            two = jnp.dot(
                pown[...], wbuf[:, pl.ds(pl.multiple_of(k * 256, 256), 256)], preferred_element_type=jnp.float32
            )
            part[2 * k] = two[:, :128]
            part[2 * k + 1] = two[:, 128:]

        def ring(s, h, tmp, buf, ssem, rsem, to):
            rows = pl.ds(h * HALF, HALF)
            return remote(tmp.at[s, rows], buf.at[s, rows], ssem.at[0], rsem.at[s, h], (g, d, to))

        def hop(s, h, chunk, tmp, buf, ssem, rsem, to):
            rows = pl.ds(h * HALF, HALF)
            mine = part[chunk, rows]
            if s > 0:
                ring(s - 1, h, tmp, buf, ssem, rsem, to).wait_recv()
                mine = mine + buf[s - 1, rows].astype(jnp.float32)
            tmp[s, rows] = mine.astype(jnp.bfloat16)
            ring(s, h, tmp, buf, ssem, rsem, to).start()

        for s in range(8):
            for h in range(2):
                hop(s, h, lax.rem(m + 8 - s, N_MP), rtmp, rbuf, rr_s, rr_r, right)
                if s < 7:
                    hop(s, h, lax.rem(m + 9 + s, N_MP), ltmp, lbuf, rl_s, rl_r, left)
            if s == 2:
                send_parts()
        for h in range(2):
            ring(6, h, ltmp, lbuf, rl_s, rl_r, left).wait_recv()
            ring(7, h, rtmp, rbuf, rr_s, rr_r, right).wait_recv()
        cfin[...] = (part[m] + rbuf[7].astype(jnp.float32) + lbuf[6].astype(jnp.float32)).astype(jnp.bfloat16)

        def send_c(to, j):
            _, _, count, base, per, at = PARTS[core][j]
            return remote(
                cfin.at[pl.ds(at, count)], cbuf.at[pl.ds(pl.multiple_of(base + d * per, 16), count)],
                c_s.at[0], c_r.at[0], (2 + core, to, m),
            )

        for k, y in ((2, 0), (0, 1), (1, 0), (3, 1), (0, 0), (2, 1), (1, 1), (3, 0)):
            for j in range(2):
                send_c(lax.rem(y_hi + y, 2) * 4 + lax.rem(x + k, 4), j).start()

        kv_out[...] = jnp.zeros_like(kv_out)
        rows_out[...] = jnp.zeros_like(rows_out)

        def all_sent(ref, rows, sem):
            remote(ref.at[pl.ds(0, rows)], ref.at[pl.ds(0, rows)], sem.at[0], c_r.at[0], (2 + core, d, m)).wait_send()

        all_sent(pbuf, 4 * PART_ROWS[core], p_s)
        all_sent(rtmp, 8, rr_s)
        all_sent(ltmp, 7, rl_s)
        all_sent(cbuf, N_DP * PART_ROWS[core], c_s)

    @pl.when(g == 0)
    def _():
        encoder(0, aud_ref, abuf, again_hbm, again_ref, AW, aslot, araw, aslot_r)

    @pl.when(g == 1)
    def _():
        encoder(1, img_ref, ibuf, igain_hbm, igain_ref, IW, islot, iraw, islot_r)

    def backbone(core):
        me = core * N_DP + d
        own = []
        for k, (src, count, base) in enumerate(((ap_ref, 160, 0), (ip_ref, 400, AW))):
            one = pltpu.make_async_copy(
                src, pbuf.at[pl.ds(pl.multiple_of(base + d * count, 16), count)], lsem.at[k]
            )
            one.start()
            own.append(one)
        for one in tables:
            one.wait()
        picks = []
        for s in range(2):
            found = jnp.int32(0)
            first = jnp.int32(0)
            second = jnp.int32(0)
            for e in range(N_DP):
                hit = dest_ref[s, 0, e] == me
                for b in range(1, BLOCKS):
                    hit = hit | (dest_ref[s, b, e] == me)
                first = jnp.where(hit & (found == 0), e, first)
                second = jnp.where(hit & (found == 1), e, second)
                found = found + jnp.where(hit, 1, 0)
            picks.append((first, second))
        pl.semaphore_wait(barrier, GREETED)

        which, row, count, _, _, _ = PARTS[core][1]
        to_relay = remote(
            (ap_ref, ip_ref)[which].at[pl.ds(row, count)], prel.at[pl.ds(0, count)], rel_s.at[0], rel_r.at[0],
            (core, (1 - y_hi) * 4 + x, m),
        )
        to_relay.start()

        def pick_rows(s, raw, sem, lo, width):
            remote(raw, raw, slot_s.at[0], sem.at[0], (0, d, m)).wait_recv()
            both = jnp.concatenate(
                [raw[picks[s][0]].astype(jnp.float32), raw[picks[s][1]].astype(jnp.float32)], axis=0
            )
            ag[0, :, pl.ds(lo, width)] = both.astype(jnp.bfloat16)

        def go_right(s, p):
            cols = pl.ds(*COLS[p])
            return remote(
                ag.at[(16 - s) % 16, :, cols], ag.at[15 - s, :, cols], ag_s.at[0], agr_r.at[s, p], (g, d, right)
            )

        def go_left(s, p):
            cols = pl.ds(*COLS[p])
            return remote(ag.at[s, :, cols], ag.at[s + 1, :, cols], ag_s.at[0], agl_r.at[s, p], (g, d, left))

        def goes_right(s, p):
            return s < 7 or (s == 7 and p >= LAST_LEFT)

        def goes_left(s, p):
            return s < 7 or (s == 7 and p < LAST_LEFT)

        def gather_step(s, pieces):
            for p in pieces:
                if s > 0 and goes_right(s - 1, p):
                    go_right(s - 1, p).wait_recv()
                if goes_right(s, p):
                    go_right(s, p).start()
                if s > 0 and goes_left(s - 1, p):
                    go_left(s - 1, p).wait_recv()
                if goes_left(s, p):
                    go_left(s, p).start()

        def send_part(k, j):
            which, row, count, base, per, _ = PARTS[core][j]
            return remote(
                (ap_ref, ip_ref)[which].at[pl.ds(row, count)],
                pbuf.at[pl.ds(pl.multiple_of(base + d * per, 16), count)],
                p_s.at[0], p_r.at[d], (2 + core, y_hi * 4 + lax.rem(x + k, 4), m),
            )

        def rows_of(e, core_of, j):
            _, _, count, base, per, _ = PARTS[core_of][j]
            return pl.ds(pl.multiple_of(base + e * per, 16), count)

        def forward(buf, e, core_of, j, ssem, rsem):
            rows = rows_of(e, core_of, j)
            return remote(buf.at[rows], buf.at[rows], ssem.at[0], rsem.at[0], (2 + (1 - core), d, m))

        def whole(buf, rows, ssem, rsem):
            return remote(buf.at[pl.ds(0, rows)], buf.at[pl.ds(0, rows)], ssem, rsem, (2 + (1 - core), d, m))

        def pass_on_p(e):
            whole(pbuf, PART_ROWS[core], p_s.at[0], p_r.at[e]).wait_recv()
            for j in range(2):
                forward(pbuf, e, core, j, pf_s, pf_r).start()

        pick_rows(0, araw, aslot_r, 0, AW)
        gather_step(0, AUDIO_PIECES)
        pick_rows(1, iraw, islot_r, AW, IW)
        gather_step(0, IMAGE_PIECES)
        for k in range(1, 4):
            for j in range(2):
                send_part(k, j).start()
        for s in range(1, 6):
            gather_step(s, AUDIO_PIECES)
            gather_step(s, IMAGE_PIECES)
        for k in range(1, 4):
            pass_on_p(y_hi * 4 + lax.rem(x + k, 4))
        gather_step(6, AUDIO_PIECES)
        gather_step(6, IMAGE_PIECES)
        for k in range(4):
            pass_on_p((1 - y_hi) * 4 + k)
        gather_step(7, AUDIO_PIECES)
        gather_step(7, IMAGE_PIECES)
        gather_step(8, AUDIO_PIECES)

        for one in own:
            one.wait()

        whole(pbuf, 7 * PART_ROWS[1 - core], pf_s.at[0], pf_r.at[0]).wait_recv()

        def project(s, lo, width):
            @pl.loop(0, 2)
            def _(n):
                cols = pl.ds(pl.multiple_of(n * 256, 256), 256)
                acc[pl.ds(s * 256, 256), cols] = jnp.dot(
                    ag[:, :, pl.ds(lo, width)].reshape(256, width), pbuf[pl.ds(lo, width), cols],
                    preferred_element_type=jnp.float32,
                )

        project(0, 0, AW)
        gather_step(8, IMAGE_PIECES)
        project(1, AW, IW)

        for s in range(2):
            halves = []
            for r in range(2):
                tok = acc[pl.ds(s * 256 + r * 128, 128), :].astype(jnp.bfloat16).astype(jnp.float32)
                sq = tok * tok
                sq = sq[:, :128] + sq[:, 128:256] + sq[:, 256:384] + sq[:, 384:]
                halves.append(jnp.sum(sq.T, axis=0, keepdims=True))
            line = jnp.broadcast_to(jnp.concatenate(halves, axis=1), (8, 256))
            mssrc[:, pl.ds(s * 256, 256)] = pltpu.roll(line, m * 16, 1)[:1]

        def send_ms(k):
            return remote(
                mssrc, msall.at[k], ms_s.at[0], ms_r.at[0], (g, d, lax.rem(m + k, N_MP))
            )

        for k in (8, 7, 9, 6, 10, 5, 11, 4, 12, 3, 13, 2, 14, 1, 15):
            send_ms(k).start()

        whole(cbuf, N_DP * PART_ROWS[core], c_s.at[0], c_r.at[0]).wait_recv()
        for e in range(N_DP):
            for j in range(2):
                forward(cbuf, e, core, j, cf_s, cf_r).start()

        for s in range(2):
            for rel in range(16):
                z = lax.rem(m + rel, N_MP)
                for p in range(2):
                    rows_out[2 * s + p, z] = acc[pl.ds(s * 256 + rel * 16 + p * 8, 8), :].astype(jnp.bfloat16)

        whole(cbuf, N_DP * PART_ROWS[1 - core], cf_s.at[0], cf_r.at[0]).wait_recv()
        for s, (lo, width) in enumerate(((0, AW), (AW, IW))):
            kvacc[pl.ds(s * 256, 256), :] = jnp.dot(
                ag[:, :, pl.ds(lo, width)].reshape(256, width), cbuf[pl.ds(lo, width), :],
                preferred_element_type=jnp.float32,
            )

        to_relay.wait_send()
        whole(ag, 15, ag_s.at[0], agr_r.at[0, 0]).wait_send()
        whole(pbuf, 3 * PART_ROWS[core], p_s.at[0], p_r.at[d]).wait_send()
        whole(pbuf, 7 * PART_ROWS[core], pf_s.at[0], pf_r.at[0]).wait_send()
        whole(cbuf, N_DP * PART_ROWS[core], cf_s.at[0], cf_r.at[0]).wait_send()

        all_ms = remote(
            msall.at[pl.ds(1, 15)], msall.at[pl.ds(1, 15)], ms_s.at[0], ms_r.at[0], (g, d, right)
        )
        all_ms.wait_recv()
        total = mssrc[...]
        for k in range(1, N_MP):
            total = total + msall[k]
        scale = lax.rsqrt(total / (FEAT * N_MP) + EPS_ROOT)
        for s in range(2):
            line = jnp.broadcast_to(scale[:, s * 256 : s * 256 + 256], (8, 256))
            line = pltpu.roll(line, lax.rem((N_MP - m) * 16, 256), 1)
            for r in range(2):
                col = jnp.broadcast_to(line[:1, r * 128 : r * 128 + 128], (128, 128)).T
                at = pl.ds(s * 256 + r * 128, 128)
                kvacc[at, :] = kvacc[at, :] * col
        for s in range(2):
            for rel in range(16):
                z = lax.rem(m + rel, N_MP)
                for p in range(2):
                    kv_out[2 * s + p, z] = kvacc[pl.ds(s * 256 + rel * 16 + p * 8, 8), :].astype(jnp.bfloat16)

        all_ms.wait_send()

    @pl.when(g == 2)
    def _():
        backbone(0)

    @pl.when(g == 3)
    def _():
        backbone(1)


def store(kv_in, rows_in, kv_out, rows_out, sem):
    one = pltpu.make_async_copy(rows_in, rows_out, sem.at[0])
    two = pltpu.make_async_copy(kv_in, kv_out, sem.at[1])
    one.start()
    two.start()
    one.wait()
    two.wait()


def shards(
    audio_states, image_states, audio_gain, image_gain, audio_proj, image_proj,
    block_rows, destination, input_gain, kv_weight,
):
    anywhere = pl.BlockSpec(memory_space=pl.ANY)
    vmem = pl.BlockSpec(memory_space=pltpu.VMEM)
    bf, f32 = jnp.bfloat16, jnp.float32
    dma = pltpu.SemaphoreType.DMA
    kv, rows = pl.pallas_call(
        kernel,
        out_shape=(
            pltpu.VMEM((BLOCKS, N_MP, SHARE, KVC), bf),
            pltpu.VMEM((BLOCKS, N_MP, SHARE, FEAT), bf),
        ),
        in_specs=[anywhere] * 10,
        out_specs=(vmem, vmem),
        scratch_shapes=[
            pltpu.VMEM((AW,), f32),
            pltpu.VMEM((IW,), f32),
            pltpu.VMEM((FEAT,), f32),
            pltpu.SMEM((2, BLOCKS, N_DP), jnp.int32),
            pltpu.SMEM((2, BLOCKS, N_DP), jnp.int32),
            pltpu.VMEM((32, AW), bf),
            pltpu.VMEM((32, IW), bf),
            pltpu.VMEM((BLOCKS, SHARE, IW), f32),
            pltpu.VMEM((2 * N_DP, SHARE, AW), bf),
            pltpu.VMEM((2 * N_DP, SHARE, IW), bf),
            pltpu.VMEM((N_DP, SHARE, AW), bf),
            pltpu.VMEM((N_DP, SHARE, IW), bf),
            pltpu.VMEM((N_MP, 16, KW), bf),
            pltpu.VMEM((KW, FEAT), bf),
            pltpu.VMEM((KW, KVC), bf),
            pltpu.VMEM((PART, FEAT), bf),
            pltpu.VMEM((160, FEAT), bf),
            pltpu.VMEM((FEAT, 2048), bf),
            pltpu.VMEM((N_MP, PART, KVC), f32),
            pltpu.VMEM((8, PART, KVC), bf),
            pltpu.VMEM((7, PART, KVC), bf),
            pltpu.VMEM((8, PART, KVC), bf),
            pltpu.VMEM((7, PART, KVC), bf),
            pltpu.VMEM((PART, KVC), bf),
            pltpu.VMEM((FEAT, FEAT), f32),
            pltpu.VMEM((FEAT, KVC), f32),
            pltpu.VMEM((1, FEAT), f32),
            pltpu.VMEM((N_MP, 1, FEAT), f32),
            dma((4,)),
            dma((1,)), dma((1,)), dma((1,)),
            dma((1,)), dma((8, 7)), dma((8, 7)),
            dma((1,)), dma((8,)), dma((1,)), dma((1,)),
            dma((1,)), dma((1,)), dma((1,)), dma((1,)),
            dma((1,)), dma((8, 2)), dma((1,)), dma((7, 2)),
            dma((1,)), dma((1,)), dma((1,)), dma((1,)), dma((4,)),
        ],
        compiler_params=pltpu.CompilerParams(
            collective_id=0, has_side_effects=True, vmem_limit_bytes=60 * 1024 * 1024
        ),
        name="route_project",
    )(
        audio_states, image_states, audio_gain, image_gain, audio_proj, image_proj,
        block_rows.transpose(0, 2, 1), destination.transpose(0, 2, 1), input_gain, kv_weight,
    )
    kv, rows = pl.pallas_call(
        store,
        out_shape=(
            jax.ShapeDtypeStruct((BLOCKS, N_MP, SHARE, KVC), bf),
            jax.ShapeDtypeStruct((BLOCKS, N_MP, SHARE, FEAT), bf),
        ),
        in_specs=[vmem, vmem],
        out_specs=(anywhere, anywhere),
        scratch_shapes=[dma((2,))],
        name="store",
    )(pltpu.with_memory_space_constraint(kv, pltpu.VMEM), pltpu.with_memory_space_constraint(rows, pltpu.VMEM))
    return (kv.reshape(1, BLOCKS * BLOCK, KVC), rows.reshape(1, BLOCKS * BLOCK, FEAT))


def solution(mesh):
    in_specs = (
        P("group", ("dp", "mp"), None),
        P("group", ("dp", "mp"), None),
        P(),
        P(),
        P("dp", "mp"),
        P("dp", "mp"),
        P(),
        P(),
        P("mp"),
        P("mp", None),
    )
    out_specs = (P("group", "dp", "mp"), P("group", "dp", "mp"))
    return jax.shard_map(shards, mesh=mesh, in_specs=in_specs, out_specs=out_specs, check_vma=False)
```
